32 devices in a mesh: seq: 8 (over z, core), grp: 4 (over y, x).
Axes of the slice: x: 2, y: 2, z: 4, core: 2. Of those that a mesh axis runs over, the one named last changes fastest.
Arguments:
- tokens: bfloat16 [65536, 1280], P(('seq', 'grp')), may hold values from -27 to 27
- slot_keys: bfloat16 [1280, 128], replicated, may hold values from -1.5 to 1.5
- norm_gain: float32 [32, 1280], P(('seq', 'grp')), may hold values from 0.1 to 1.9
- w_in: bfloat16 [32, 1280, 2560], P(('seq', 'grp')), may hold values from -0.15625 to 0.15625
- w_out: bfloat16 [32, 2560, 1280], P(('seq', 'grp')), may hold values from -0.125 to 0.125
Outputs:
- mixed: bfloat16 [65536, 1280], P(('seq', 'grp'))
The draws below stay inside these ranges and needn't reach their ends.
All inputs are finite; a program needn't handle non-finite values.
Results may differ from the reference program's by a relative error of at most 0.007.
Values may be sent and summed in bfloat16 or wider, within the bound.
No kernel may reach another device: no remote copies, remote signals or barrier semaphores. Data moves between devices by JAX's collectives and lax.ppermute only.
A program may use at most 128 MiB of HBM per device.

```python
import jax
import jax.numpy as jnp
from jax import lax

D = 1280
FF = 2560
SLOTS_PER = 4
TOK_DEV = 2048
EXPERTS = 32
SLOTS = 128
TOKENS = 65536


def slot_table(key):
    sub = jax.random.fold_in(key, 7)
    table = jax.random.normal(sub, (D, SLOTS), jnp.float32) * (3.0 / jnp.sqrt(jnp.float32(D)))
    return jnp.clip(table, -1.5, 1.5)


def draw_slot_keys(key, part):
    return slot_table(key).astype(jnp.bfloat16)


def draw_tokens(key, part):
    base = jnp.clip(jax.random.normal(jax.random.fold_in(key, 11), (TOKENS, D), jnp.float32), -6.0, 6.0)
    bound = 24.0 + 4000 // D
    return jnp.clip(base, -bound, bound).astype(jnp.bfloat16)


def level_of(stream_key, shape, cuts, low, top_value):
    factor_of = 1.0
    for position, parts in cuts:
        heights = jax.random.uniform(jax.random.fold_in(jax.random.fold_in(stream_key, 6), position), (parts,), jnp.float32, low / len(cuts), top_value / len(cuts))
        factor_of = factor_of * jnp.repeat(jnp.exp(heights), shape[position] // parts).reshape((-1,) + (1,) * (len(shape) - 1 - position))
    return factor_of


def centred(rng, shape, spread, most, shards=(), held_as=jnp.bfloat16):
    values = spread * jax.random.normal(rng, shape, jnp.float32)
    if shards:
        values = values * level_of(rng, shape, shards, -0.22, 0.18)
    return jnp.clip(values, -most, most).astype(held_as)


def setup_inputs(seed: int = 0) -> dict:
    key_of = jax.random.split(jax.random.key(seed), 6)
    return {
        "tokens": draw_tokens(jax.random.fold_in(key_of[5], 71), 0),
        "slot_keys": draw_slot_keys(jax.random.fold_in(key_of[5], 71), 0),
        "norm_gain": jnp.clip(1.0 + 0.18 * jax.random.normal(key_of[2], (EXPERTS, D), jnp.float32), 0.1, 1.9),
        "w_in": centred(key_of[3], (EXPERTS, D, FF), D ** -0.5, 0.15625, ((0, 32),)),
        "w_out": centred(key_of[4], (EXPERTS, FF, D), FF ** -0.5, 0.125, ((0, 32),)),
    }


def reference(tokens, slot_keys, norm_gain, w_in, w_out):
    blocks = tokens.reshape(TOKENS // TOK_DEV, TOK_DEV, D)

    def dispatch_step(carry, block):
        top, numer, total = carry
        logits = jnp.dot(block, slot_keys, preferred_element_type=jnp.float32)
        peak = jnp.max(logits, axis=0)
        scores = jnp.exp(logits - peak[None, :])
        weights = scores.astype(jnp.bfloat16)
        part = jnp.dot(weights.T, block, preferred_element_type=jnp.float32)
        newtop = jnp.maximum(top, peak)
        older = jnp.exp(top - newtop)
        newer = jnp.exp(peak - newtop)
        numer = numer * older[:, None] + part * newer[:, None]
        total = total * older + jnp.sum(scores, axis=0) * newer
        return (newtop, numer, total), None

    start = (jnp.full((SLOTS,), -jnp.inf, jnp.float32), jnp.zeros((SLOTS, D), jnp.float32), jnp.zeros((SLOTS,), jnp.float32))
    (top, numer, total), unused = lax.scan(dispatch_step, start, blocks)
    slot_in = (numer / total[:, None]).reshape(EXPERTS, SLOTS_PER, D)
    normed = (slot_in * norm_gain[:, None, :]).astype(jnp.bfloat16)

    def expert_step(items):
        rows, first, second = items
        hidden = jax.nn.gelu(jnp.dot(rows, first, preferred_element_type=jnp.float32)).astype(jnp.bfloat16)
        return jnp.dot(hidden, second, preferred_element_type=jnp.float32).astype(jnp.bfloat16)

    expert_out = lax.map(expert_step, (normed, w_in, w_out)).reshape(SLOTS, D)

    def combine_step(block):
        logits = jnp.dot(block, slot_keys, preferred_element_type=jnp.float32)
        row_top = jnp.max(logits, axis=1, keepdims=True)
        row_exp = jnp.exp(logits - row_top)
        combine = (row_exp / jnp.sum(row_exp, axis=1, keepdims=True)).astype(jnp.bfloat16)
        return jnp.dot(combine, expert_out, preferred_element_type=jnp.float32).astype(jnp.bfloat16)

    mixed = lax.map(combine_step, blocks)
    return mixed.reshape(TOKENS, D)
```

```python
import functools

import jax
import jax.numpy as jnp
from jax import lax
from jax.experimental import pallas as pl
from jax.experimental.pallas import tpu as pltpu
from jax.sharding import PartitionSpec as P

AXES = ("seq", "grp")
LANES = 128
TILE = 256
COLS = 256


def split3(x):
    hi = x.astype(jnp.bfloat16)
    rest = x - hi.astype(jnp.float32)
    mid = rest.astype(jnp.bfloat16)
    low = (rest - mid.astype(jnp.float32)).astype(jnp.bfloat16)
    return hi, mid, low


def dispatch_kernel(devices, tok_hbm, keys_hbm, msg_ref, logits_ref, tok, keys, wt, tok_sem, key_sem):
    rows, width = tok.shape
    slots = keys.shape[1]
    per_dev = slots // devices
    tiles = rows // TILE

    def tok_copy(i):
        part = pl.ds(i * TILE, TILE)
        return pltpu.make_async_copy(tok_hbm.at[part], tok.at[part], tok_sem.at[i])

    key_copy = pltpu.make_async_copy(keys_hbm, keys, key_sem)
    key_copy.start()
    for i in range(tiles):
        tok_copy(i).start()
    key_copy.wait()
    peak8 = jnp.full((8, slots), -jnp.inf, jnp.float32)
    for i in range(tiles):
        tok_copy(i).wait()
        part = pl.ds(i * TILE, TILE)
        logits = jnp.dot(tok[part, :], keys[...], preferred_element_type=jnp.float32)
        logits_ref[part, :] = logits
        peak8 = jnp.maximum(peak8, jnp.max(logits.reshape(TILE // 8, 8, slots), axis=0))
    peak = jnp.max(peak8, axis=0, keepdims=True)
    total8 = jnp.zeros((8, slots), jnp.float32)
    for i in range(tiles):
        part = pl.ds(i * TILE, TILE)
        scores = jnp.exp(logits_ref[part, :] - peak)
        total8 = total8 + jnp.sum(scores.reshape(TILE // 8, 8, slots), axis=0)
        wt[:, part] = scores.astype(jnp.bfloat16).T
    total = jnp.sum(total8, axis=0, keepdims=True)
    for n in range(width // COLS):
        part = pl.ds(n * COLS, COLS)
        numer = jnp.dot(wt[...], tok[:, part], preferred_element_type=jnp.float32)
        for d in range(devices):
            msg_ref[d, :, part] = numer[d * per_dev : (d + 1) * per_dev].astype(jnp.bfloat16)
    stats = [*split3(peak), *split3(total)]
    stats = [s.astype(jnp.float32) for s in stats]
    stats = jnp.concatenate(stats + [jnp.zeros((LANES - len(stats), slots), jnp.float32)], axis=0)
    for b in range(slots // LANES):
        block = stats[:, b * LANES : (b + 1) * LANES].T
        for d in range(LANES // per_dev):
            msg_ref[b * (LANES // per_dev) + d, :, width:] = block[d * per_dev : (d + 1) * per_dev].astype(jnp.bfloat16)


def dispatch(devices, tokens, keys):
    rows, width = tokens.shape
    slots = keys.shape[1]
    per_dev = slots // devices
    return pl.pallas_call(
        functools.partial(dispatch_kernel, devices),
        out_shape=(
            jax.ShapeDtypeStruct((devices, per_dev, width + LANES), jnp.bfloat16),
            jax.ShapeDtypeStruct((rows, slots), jnp.float32),
        ),
        in_specs=[pl.BlockSpec(memory_space=pltpu.HBM)] * 2,
        out_specs=[pl.BlockSpec(memory_space=pltpu.VMEM)] * 2,
        scratch_shapes=[
            pltpu.VMEM((rows, width), jnp.bfloat16),
            pltpu.VMEM(keys.shape, jnp.bfloat16),
            pltpu.VMEM((slots, rows), jnp.bfloat16),
            pltpu.SemaphoreType.DMA((rows // TILE,)),
            pltpu.SemaphoreType.DMA,
        ],
        name="dispatch",
        compiler_params=pltpu.CompilerParams(vmem_limit_bytes=32 << 20),
        cost_estimate=pl.CostEstimate(
            flops=4 * rows * width * slots,
            bytes_accessed=2 * rows * width,
            transcendentals=rows * slots,
        ),
    )(tokens, keys)


def expert_kernel(copies, recv_ref, gain_ref, w_in_hbm, w_out_hbm, out_ref, w_in, w_out, in_sem, out_sem):
    devices, per_dev, wide = recv_ref.shape
    width, hidden = w_in.shape
    step = 512
    n_in, n_out = hidden // step, width // COLS

    def in_copy(i):
        part = pl.ds(i * step, step)
        return pltpu.make_async_copy(w_in_hbm.at[0, :, part], w_in.at[:, part], in_sem.at[i])

    def out_copy(i):
        part = pl.ds(i * step, step)
        return pltpu.make_async_copy(w_out_hbm.at[0, part], w_out.at[part], out_sem.at[i])

    for i in range(n_in):
        in_copy(i).start()
    for i in range(n_in):
        out_copy(i).start()

    stats = recv_ref[:, :, width:].astype(jnp.float32)
    peaks = stats[:, :, 0:1] + stats[:, :, 1:2] + stats[:, :, 2:3]
    totals = stats[:, :, 3:4] + stats[:, :, 4:5] + stats[:, :, 5:6]
    factor = jnp.exp(peaks - jnp.max(peaks, axis=0, keepdims=True))
    own_total = jnp.sum(totals * factor, axis=0)
    numer = jnp.zeros((per_dev, width), jnp.float32)
    for d in range(devices):
        numer = numer + recv_ref[d, :, :width].astype(jnp.float32) * factor[d]
    normed = (numer / own_total * gain_ref[...]).astype(jnp.bfloat16)
    parts = []
    for i in range(n_in):
        in_copy(i).wait()
        parts.append(jnp.dot(normed, w_in[:, i * step : (i + 1) * step], preferred_element_type=jnp.float32))
    acc = jnp.zeros((per_dev, width), jnp.float32)
    for i in range(n_in):
        act = jax.nn.gelu(parts[i]).astype(jnp.bfloat16)
        out_copy(i).wait()
        acc = acc + jnp.dot(act, w_out[i * step : (i + 1) * step, :], preferred_element_type=jnp.float32)
    res = acc.astype(jnp.bfloat16)
    for d in range(copies):
        out_ref[d] = res


def experts(copies, recv, gain, w_in, w_out):
    devices, per_dev, wide = recv.shape
    width, hidden = w_in.shape[1:]
    steps = hidden // 512
    return pl.pallas_call(
        functools.partial(expert_kernel, copies),
        out_shape=jax.ShapeDtypeStruct((copies, per_dev, width), jnp.bfloat16),
        in_specs=[pl.BlockSpec(memory_space=pltpu.VMEM)] * 2 + [pl.BlockSpec(memory_space=pltpu.HBM)] * 2,
        out_specs=pl.BlockSpec(memory_space=pltpu.VMEM),
        scratch_shapes=[
            pltpu.VMEM((width, hidden), jnp.bfloat16),
            pltpu.VMEM((hidden, width), jnp.bfloat16),
            pltpu.SemaphoreType.DMA((steps,)),
            pltpu.SemaphoreType.DMA((steps,)),
        ],
        name="experts",
        compiler_params=pltpu.CompilerParams(vmem_limit_bytes=32 << 20),
        cost_estimate=pl.CostEstimate(
            flops=4 * per_dev * width * hidden,
            bytes_accessed=4 * width * hidden,
            transcendentals=per_dev * hidden,
        ),
    )(recv, gain, w_in, w_out)


def mix_kernel(logits_ref, rows_ref, out_ref, table):
    per_dev = rows_ref.shape[1]

    @pl.when(pl.program_id(0) == 0)
    def _():
        table[...] = rows_ref[...].reshape(table.shape)

    logits = logits_ref[...]
    row_exp = jnp.exp(logits - jnp.max(logits, axis=1, keepdims=True))
    combine = (row_exp / jnp.sum(row_exp, axis=1, keepdims=True)).astype(jnp.bfloat16)
    out_ref[...] = jnp.dot(combine, table[...], preferred_element_type=jnp.float32).astype(jnp.bfloat16)


def mix(logits, gathered):
    rows, slots = logits.shape
    width = gathered.shape[2]
    return pl.pallas_call(
        mix_kernel,
        grid=(rows // TILE,),
        out_shape=jax.ShapeDtypeStruct((rows, width), jnp.bfloat16),
        in_specs=[
            pl.BlockSpec((TILE, slots), lambda i: (i, 0)),
            pl.BlockSpec(gathered.shape, lambda i: (0, 0, 0)),
        ],
        out_specs=pl.BlockSpec((TILE, width), lambda i: (i, 0)),
        scratch_shapes=[pltpu.VMEM((slots, width), jnp.bfloat16)],
        name="mix",
        compiler_params=pltpu.CompilerParams(vmem_limit_bytes=32 << 20),
    )(logits, gathered)


def on_device(tokens, slot_keys, norm_gain, w_in, w_out):
    devices = lax.axis_size(AXES)
    message, logits = dispatch(devices, tokens, slot_keys)
    received = lax.all_to_all(message, AXES, split_axis=0, concat_axis=0, tiled=True)
    copies = experts(devices, received, norm_gain, w_in, w_out)
    gathered = lax.all_to_all(copies, AXES, split_axis=0, concat_axis=0, tiled=True)
    return mix(logits, gathered)


def solution(mesh):
    return jax.shard_map(
        on_device,
        mesh=mesh,
        in_specs=(
            P(AXES, None),
            P(),
            P(AXES, None),
            P(AXES, None, None),
            P(AXES, None, None),
        ),
        out_specs=P(AXES, None),
        check_vma=False,
    )
```

```python
import functools

import jax
import jax.numpy as jnp
from jax import lax
from jax.experimental import pallas as pl
from jax.experimental.pallas import tpu as pltpu
from jax.sharding import PartitionSpec as P

AXES = ("seq", "grp")
LANES = 128
TILE = 256
COLS = 256
DEPTH = 640
CHUNK = 1024


def in_hbm(x):
    return pltpu.with_memory_space_constraint(x, pltpu.HBM)


def split3(x):
    hi = x.astype(jnp.bfloat16)
    rest = x - hi.astype(jnp.float32)
    mid = rest.astype(jnp.bfloat16)
    low = (rest - mid.astype(jnp.float32)).astype(jnp.bfloat16)
    return hi, mid, low


def dispatch_kernel(devices, tok_hbm, keys_hbm, msg_ref, logits_ref, tok, keys, wt, tok_sem, key_sem):
    rows, width = tok.shape
    slots = keys.shape[1]
    per_dev = slots // devices
    tiles = rows // TILE
    chunks = rows // CHUNK

    def tok_copy(i):
        part = pl.ds(i * CHUNK, CHUNK)
        return pltpu.make_async_copy(tok_hbm.at[part], tok.at[part], tok_sem.at[i])

    key_copy = pltpu.make_async_copy(keys_hbm, keys, key_sem)
    key_copy.start()
    for i in range(chunks):
        tok_copy(i).start()
    key_copy.wait()
    peak8 = jnp.full((8, slots), -jnp.inf, jnp.float32)
    for i in range(tiles):
        if i * TILE % CHUNK == 0:
            tok_copy(i * TILE // CHUNK).wait()
        part = pl.ds(i * TILE, TILE)
        logits = jnp.dot(tok[part, :], keys[...], preferred_element_type=jnp.float32)
        logits_ref[part, :] = logits
        peak8 = jnp.maximum(peak8, jnp.max(logits.reshape(TILE // 8, 8, slots), axis=0))
    peak = jnp.max(peak8, axis=0, keepdims=True)
    total8 = jnp.zeros((8, slots), jnp.float32)
    for i in range(tiles):
        part = pl.ds(i * TILE, TILE)
        scores = jnp.exp(logits_ref[part, :] - peak)
        total8 = total8 + jnp.sum(scores.reshape(TILE // 8, 8, slots), axis=0)
        wt[:, part] = scores.astype(jnp.bfloat16).T
    total = jnp.sum(total8, axis=0, keepdims=True)
    for n in range(width // COLS):
        part = pl.ds(n * COLS, COLS)
        numer = jnp.dot(wt[...], tok[:, part], preferred_element_type=jnp.float32)
        for d in range(devices):
            msg_ref[d, :, part] = numer[d * per_dev : (d + 1) * per_dev].astype(jnp.bfloat16)
    stats = [*split3(peak), *split3(total)]
    stats = [s.astype(jnp.float32) for s in stats]
    stats = jnp.concatenate(stats + [jnp.zeros((LANES - len(stats), slots), jnp.float32)], axis=0)
    for b in range(slots // LANES):
        block = stats[:, b * LANES : (b + 1) * LANES].T
        for d in range(LANES // per_dev):
            msg_ref[b * (LANES // per_dev) + d, :, width:] = block[d * per_dev : (d + 1) * per_dev].astype(jnp.bfloat16)


def dispatch(devices, tokens, keys):
    rows, width = tokens.shape
    slots = keys.shape[1]
    per_dev = slots // devices
    return pl.pallas_call(
        functools.partial(dispatch_kernel, devices),
        out_shape=(
            jax.ShapeDtypeStruct((devices, per_dev, width + LANES), jnp.bfloat16),
            jax.ShapeDtypeStruct((rows, slots), jnp.float32),
        ),
        in_specs=[pl.BlockSpec(memory_space=pltpu.HBM)] * 2,
        out_specs=[pl.BlockSpec(memory_space=pltpu.VMEM)] * 2,
        scratch_shapes=[
            pltpu.VMEM((rows, width), jnp.bfloat16),
            pltpu.VMEM(keys.shape, jnp.bfloat16),
            pltpu.VMEM((slots, rows), jnp.bfloat16),
            pltpu.SemaphoreType.DMA((rows // CHUNK,)),
            pltpu.SemaphoreType.DMA,
        ],
        name="dispatch",
        compiler_params=pltpu.CompilerParams(vmem_limit_bytes=32 << 20),
        cost_estimate=pl.CostEstimate(
            flops=4 * rows * width * slots,
            bytes_accessed=2 * rows * width,
            transcendentals=rows * slots,
        ),
    )(in_hbm(tokens), in_hbm(keys))


def combine_kernel(logits_ref, combine_ref):
    for i in range(logits_ref.shape[0] // TILE):
        part = pl.ds(i * TILE, TILE)
        logits = logits_ref[part, :]
        row_exp = jnp.exp(logits - jnp.max(logits, axis=1, keepdims=True))
        combine_ref[part, :] = (row_exp / jnp.sum(row_exp, axis=1, keepdims=True)).astype(jnp.bfloat16)


def combining(logits):
    return pl.pallas_call(
        combine_kernel,
        out_shape=jax.ShapeDtypeStruct(logits.shape, jnp.bfloat16),
        in_specs=[pl.BlockSpec(memory_space=pltpu.VMEM)],
        out_specs=pl.BlockSpec(memory_space=pltpu.VMEM),
        name="combining",
        compiler_params=pltpu.CompilerParams(vmem_limit_bytes=32 << 20),
        cost_estimate=pl.CostEstimate(
            flops=8 * logits.size, bytes_accessed=6 * logits.size, transcendentals=logits.size
        ),
    )(logits)


def expert_kernel(copies, recv_ref, gain_hbm, w_in_hbm, w_out_hbm, out_ref, gain, w_in, w_out, gain_sem, in_sem, out_sem):
    devices, per_dev, wide = recv_ref.shape
    width, hidden = w_in.shape
    n_in, n_out = width // DEPTH, hidden // DEPTH

    def in_copy(i):
        part = pl.ds(i * DEPTH, DEPTH)
        return pltpu.make_async_copy(w_in_hbm.at[0, part], w_in.at[part], in_sem.at[i])

    def out_copy(i):
        part = pl.ds(i * DEPTH, DEPTH)
        return pltpu.make_async_copy(w_out_hbm.at[0, part], w_out.at[part], out_sem.at[i])

    gain_copy = pltpu.make_async_copy(gain_hbm, gain, gain_sem)
    gain_copy.start()
    for i in range(n_in):
        in_copy(i).start()
    for i in range(n_out):
        out_copy(i).start()

    stats = recv_ref[:, :, width:].astype(jnp.float32)
    peaks = stats[:, :, 0:1] + stats[:, :, 1:2] + stats[:, :, 2:3]
    totals = stats[:, :, 3:4] + stats[:, :, 4:5] + stats[:, :, 5:6]
    factor = jnp.exp(peaks - jnp.max(peaks, axis=0, keepdims=True))
    own_total = jnp.sum(totals * factor, axis=0)
    numer = jnp.zeros((per_dev, width), jnp.float32)
    for d in range(devices):
        numer = numer + recv_ref[d, :, :width].astype(jnp.float32) * factor[d]
    gain_copy.wait()
    normed = (numer / own_total * gain[...]).astype(jnp.bfloat16)
    pre = jnp.zeros((per_dev, hidden), jnp.float32)
    for i in range(n_in):
        part = slice(i * DEPTH, (i + 1) * DEPTH)
        in_copy(i).wait()
        pre = pre + jnp.dot(normed[:, part], w_in[part, :], preferred_element_type=jnp.float32)
    act = jax.nn.gelu(pre).astype(jnp.bfloat16)
    acc = jnp.zeros((per_dev, width), jnp.float32)
    for i in range(n_out):
        part = slice(i * DEPTH, (i + 1) * DEPTH)
        out_copy(i).wait()
        acc = acc + jnp.dot(act[:, part], w_out[part, :], preferred_element_type=jnp.float32)
    res = acc.astype(jnp.bfloat16)
    for d in range(copies):
        out_ref[d] = res


def experts(copies, recv, gain, w_in, w_out):
    devices, per_dev, wide = recv.shape
    width, hidden = w_in.shape[1:]
    return pl.pallas_call(
        functools.partial(expert_kernel, copies),
        out_shape=jax.ShapeDtypeStruct((copies, per_dev, width), jnp.bfloat16),
        in_specs=[pl.BlockSpec(memory_space=pltpu.VMEM)] + [pl.BlockSpec(memory_space=pltpu.HBM)] * 3,
        out_specs=pl.BlockSpec(memory_space=pltpu.VMEM),
        scratch_shapes=[
            pltpu.VMEM(gain.shape, gain.dtype),
            pltpu.VMEM((width, hidden), jnp.bfloat16),
            pltpu.VMEM((hidden, width), jnp.bfloat16),
            pltpu.SemaphoreType.DMA,
            pltpu.SemaphoreType.DMA((width // DEPTH,)),
            pltpu.SemaphoreType.DMA((hidden // DEPTH,)),
        ],
        name="experts",
        compiler_params=pltpu.CompilerParams(vmem_limit_bytes=32 << 20),
        cost_estimate=pl.CostEstimate(
            flops=4 * per_dev * width * hidden,
            bytes_accessed=4 * width * hidden,
            transcendentals=per_dev * hidden,
        ),
    )(recv, in_hbm(gain), in_hbm(w_in), in_hbm(w_out))


def mix_kernel(combine_ref, rows_ref, out_hbm, table, out, sems):
    rows, width = out.shape
    table[...] = rows_ref[...].reshape(table.shape)
    copies = []
    for i in range(rows // TILE):
        part = pl.ds(i * TILE, TILE)
        for n in range(width // COLS):
            cols = pl.ds(n * COLS, COLS)
            mixed = jnp.dot(combine_ref[part, :], table[:, cols], preferred_element_type=jnp.float32)
            out[part, cols] = mixed.astype(jnp.bfloat16)
        copies.append(pltpu.make_async_copy(out.at[part], out_hbm.at[part], sems.at[i]))
        copies[-1].start()
    for copy in copies:
        copy.wait()


def mix(combine, gathered):
    rows, slots = combine.shape
    width = gathered.shape[2]
    return pl.pallas_call(
        mix_kernel,
        out_shape=jax.ShapeDtypeStruct((rows, width), jnp.bfloat16),
        in_specs=[pl.BlockSpec(memory_space=pltpu.VMEM)] * 2,
        out_specs=pl.BlockSpec(memory_space=pltpu.HBM),
        scratch_shapes=[
            pltpu.VMEM((slots, width), jnp.bfloat16),
            pltpu.VMEM((rows, width), jnp.bfloat16),
            pltpu.SemaphoreType.DMA((rows // TILE,)),
        ],
        name="mix",
        compiler_params=pltpu.CompilerParams(vmem_limit_bytes=32 << 20),
        cost_estimate=pl.CostEstimate(
            flops=2 * rows * slots * width, bytes_accessed=2 * rows * width, transcendentals=0
        ),
    )(combine, gathered)


def on_device(tokens, slot_keys, norm_gain, w_in, w_out):
    devices = lax.axis_size(AXES)
    message, logits = dispatch(devices, tokens, slot_keys)
    received = lax.all_to_all(message, AXES, split_axis=0, concat_axis=0, tiled=True)
    combine = combining(logits)
    copies = experts(devices, received, norm_gain, w_in, w_out)
    gathered = lax.all_to_all(copies, AXES, split_axis=0, concat_axis=0, tiled=True)
    return mix(combine, gathered)


def solution(mesh):
    return jax.shard_map(
        on_device,
        mesh=mesh,
        in_specs=(
            P(AXES, None),
            P(),
            P(AXES, None),
            P(AXES, None, None),
            P(AXES, None, None),
        ),
        out_specs=P(AXES, None),
        check_vma=False,
    )
```

```python
import functools

import jax
import jax.numpy as jnp
from jax import lax
from jax.experimental import pallas as pl
from jax.experimental.pallas import tpu as pltpu
from jax.sharding import PartitionSpec as P

SPLIT = ("far", "core", "grp")
SAME_CORE = ("far", "grp")
CORES = 2
LANES = 128
TILE = 256
COLS = 256
DEPTH = 640
CHUNK = 1024


def in_hbm(x):
    return pltpu.with_memory_space_constraint(x, pltpu.HBM)


def split3(x):
    hi = x.astype(jnp.bfloat16)
    rest = x - hi.astype(jnp.float32)
    mid = rest.astype(jnp.bfloat16)
    low = (rest - mid.astype(jnp.float32)).astype(jnp.bfloat16)
    return hi, mid, low


def half_rows(half, slots, groups):
    size = slots // (CORES * groups)
    return [pl.ds(pl.multiple_of((g * CORES + half) * size, size), size) for g in range(groups)]


def parts_of(peak, total):
    return [p.astype(jnp.float32) for p in (*split3(peak), *split3(total))]


def stats_of(block):
    peak = block[..., 0:1] + block[..., 1:2] + block[..., 2:3]
    total = block[..., 3:4] + block[..., 4:5] + block[..., 5:6]
    return peak, total


def dispatch_kernel(groups, tok_hbm, keys_hbm, send_ref, keep_ref, logits_ref, tok, keys, wt, whole, tok_sem, key_sem):
    rows, width = tok.shape
    slots = keys.shape[1]
    tiles = rows // TILE
    chunks = rows // CHUNK

    def tok_copy(i):
        part = pl.ds(i * CHUNK, CHUNK)
        return pltpu.make_async_copy(tok_hbm.at[part], tok.at[part], tok_sem.at[i])

    key_copy = pltpu.make_async_copy(keys_hbm, keys, key_sem)
    key_copy.start()
    for i in range(chunks):
        tok_copy(i).start()
    key_copy.wait()
    peak8 = jnp.full((8, slots), -jnp.inf, jnp.float32)
    for i in range(tiles):
        if i * TILE % CHUNK == 0:
            tok_copy(i * TILE // CHUNK).wait()
        part = pl.ds(i * TILE, TILE)
        logits = jnp.dot(tok[part, :], keys[...], preferred_element_type=jnp.float32)
        logits_ref[part, :] = logits
        peak8 = jnp.maximum(peak8, jnp.max(logits.reshape(TILE // 8, 8, slots), axis=0))
    peak = jnp.max(peak8, axis=0, keepdims=True)
    total8 = jnp.zeros((8, slots), jnp.float32)
    for i in range(tiles):
        part = pl.ds(i * TILE, TILE)
        scores = jnp.exp(logits_ref[part, :] - peak)
        total8 = total8 + jnp.sum(scores.reshape(TILE // 8, 8, slots), axis=0)
        wt[:, part] = scores.astype(jnp.bfloat16).T
    total = jnp.sum(total8, axis=0, keepdims=True)
    stats = parts_of(peak, total)
    stats = jnp.concatenate(stats + [jnp.zeros((LANES - len(stats), slots), jnp.float32)], axis=0)
    for b in range(slots // LANES):
        part = slice(b * LANES, (b + 1) * LANES)
        whole[part, width:] = stats[:, part].T
    for n in range(width // COLS):
        part = pl.ds(n * COLS, COLS)
        whole[:, part] = jnp.dot(wt[...], tok[:, part], preferred_element_type=jnp.float32)
    core = lax.axis_index("core")
    size = slots // (CORES * groups)
    mine, other = half_rows(core, slots, groups), half_rows(1 - core, slots, groups)
    for g in range(groups):
        part = pl.ds(g * size, size)
        send_ref[part, :] = whole[other[g], :].astype(jnp.bfloat16)
        keep_ref[part, :] = whole[mine[g], :]


def dispatch(groups, tokens, keys):
    rows, width = tokens.shape
    slots = keys.shape[1]
    half = slots // CORES
    return pl.pallas_call(
        functools.partial(dispatch_kernel, groups),
        out_shape=(
            jax.ShapeDtypeStruct((half, width + LANES), jnp.bfloat16),
            jax.ShapeDtypeStruct((half, width + LANES), jnp.float32),
            jax.ShapeDtypeStruct((rows, slots), jnp.float32),
        ),
        in_specs=[pl.BlockSpec(memory_space=pltpu.HBM)] * 2,
        out_specs=[pl.BlockSpec(memory_space=pltpu.VMEM)] * 3,
        scratch_shapes=[
            pltpu.VMEM((rows, width), jnp.bfloat16),
            pltpu.VMEM(keys.shape, jnp.bfloat16),
            pltpu.VMEM((slots, rows), jnp.bfloat16),
            pltpu.VMEM((slots, width + LANES), jnp.float32),
            pltpu.SemaphoreType.DMA((rows // CHUNK,)),
            pltpu.SemaphoreType.DMA,
        ],
        name="dispatch",
        compiler_params=pltpu.CompilerParams(vmem_limit_bytes=32 << 20),
        cost_estimate=pl.CostEstimate(
            flops=4 * rows * width * slots,
            bytes_accessed=2 * rows * width,
            transcendentals=rows * slots,
        ),
    )(in_hbm(tokens), in_hbm(keys))


def merge_kernel(keep_ref, got_ref, msg_ref):
    peers, per_dev, wide = msg_ref.shape
    width = wide - LANES
    size = 16
    lane = lax.broadcasted_iota(jnp.int32, (size, LANES), 1)
    for b in range(keep_ref.shape[0] // size):
        rows = pl.ds(b * size, size)
        keep_peak, keep_total = stats_of(keep_ref[rows, width:])
        got_peak, got_total = stats_of(got_ref[rows, width:].astype(jnp.float32))
        peak = jnp.maximum(keep_peak, got_peak)
        keep_factor, got_factor = jnp.exp(keep_peak - peak), jnp.exp(got_peak - peak)
        total = keep_factor * keep_total + got_factor * got_total
        numer = keep_factor * keep_ref[rows, :width] + got_factor * got_ref[rows, :width].astype(jnp.float32)
        stats = jnp.zeros((size, LANES), jnp.float32)
        for i, p in enumerate(parts_of(peak, total)):
            stats = jnp.where(lane == i, p, stats)
        for d in range(size // per_dev):
            part = slice(d * per_dev, (d + 1) * per_dev)
            msg_ref[b * (size // per_dev) + d, :, :width] = numer[part].astype(jnp.bfloat16)
            msg_ref[b * (size // per_dev) + d, :, width:] = stats[part].astype(jnp.bfloat16)


def merge(peers, keep, got):
    half, wide = keep.shape
    return pl.pallas_call(
        merge_kernel,
        out_shape=jax.ShapeDtypeStruct((peers, half // peers, wide), jnp.bfloat16),
        in_specs=[pl.BlockSpec(memory_space=pltpu.VMEM)] * 2,
        out_specs=pl.BlockSpec(memory_space=pltpu.VMEM),
        name="merge",
        compiler_params=pltpu.CompilerParams(vmem_limit_bytes=32 << 20),
    )(keep, got)


def combine_kernel(logits_ref, combine_ref):
    for i in range(logits_ref.shape[0] // TILE):
        part = pl.ds(i * TILE, TILE)
        logits = logits_ref[part, :]
        row_exp = jnp.exp(logits - jnp.max(logits, axis=1, keepdims=True))
        combine_ref[part, :] = (row_exp / jnp.sum(row_exp, axis=1, keepdims=True)).astype(jnp.bfloat16)


def combining(logits):
    return pl.pallas_call(
        combine_kernel,
        out_shape=jax.ShapeDtypeStruct(logits.shape, jnp.bfloat16),
        in_specs=[pl.BlockSpec(memory_space=pltpu.VMEM)],
        out_specs=pl.BlockSpec(memory_space=pltpu.VMEM),
        name="combining",
        compiler_params=pltpu.CompilerParams(vmem_limit_bytes=32 << 20),
        cost_estimate=pl.CostEstimate(
            flops=8 * logits.size, bytes_accessed=6 * logits.size, transcendentals=logits.size
        ),
    )(logits)


def expert_kernel(recv_ref, gain_hbm, w_in_hbm, w_out_hbm, out_ref, gain, w_in, w_out, gain_sem, in_sem, out_sem):
    peers, per_dev, wide = recv_ref.shape
    width, hidden = w_in.shape
    n_in, n_out = width // DEPTH, hidden // DEPTH

    def in_copy(i):
        part = pl.ds(i * DEPTH, DEPTH)
        return pltpu.make_async_copy(w_in_hbm.at[0, part], w_in.at[part], in_sem.at[i])

    def out_copy(i):
        part = pl.ds(i * DEPTH, DEPTH)
        return pltpu.make_async_copy(w_out_hbm.at[0, part], w_out.at[part], out_sem.at[i])

    gain_copy = pltpu.make_async_copy(gain_hbm, gain, gain_sem)
    gain_copy.start()
    for i in range(n_in):
        in_copy(i).start()
    for i in range(n_out):
        out_copy(i).start()

    peaks, totals = stats_of(recv_ref[:, :, width:].astype(jnp.float32))
    factor = jnp.exp(peaks - jnp.max(peaks, axis=0, keepdims=True))
    own_total = jnp.sum(totals * factor, axis=0)
    numer = jnp.zeros((per_dev, width), jnp.float32)
    for d in range(peers):
        numer = numer + recv_ref[d, :, :width].astype(jnp.float32) * factor[d]
    gain_copy.wait()
    normed = (numer / own_total * gain[...]).astype(jnp.bfloat16)
    pre = jnp.zeros((per_dev, hidden), jnp.float32)
    for i in range(n_in):
        part = slice(i * DEPTH, (i + 1) * DEPTH)
        in_copy(i).wait()
        pre = pre + jnp.dot(normed[:, part], w_in[part, :], preferred_element_type=jnp.float32)
    act = jax.nn.gelu(pre).astype(jnp.bfloat16)
    acc = jnp.zeros((per_dev, width), jnp.float32)
    for i in range(n_out):
        part = slice(i * DEPTH, (i + 1) * DEPTH)
        out_copy(i).wait()
        acc = acc + jnp.dot(act[:, part], w_out[part, :], preferred_element_type=jnp.float32)
    res = acc.astype(jnp.bfloat16)
    for d in range(peers):
        out_ref[d] = res


def experts(recv, gain, w_in, w_out):
    peers, per_dev, wide = recv.shape
    width, hidden = w_in.shape[1:]
    return pl.pallas_call(
        expert_kernel,
        out_shape=jax.ShapeDtypeStruct((peers, per_dev, width), jnp.bfloat16),
        in_specs=[pl.BlockSpec(memory_space=pltpu.VMEM)] + [pl.BlockSpec(memory_space=pltpu.HBM)] * 3,
        out_specs=pl.BlockSpec(memory_space=pltpu.VMEM),
        scratch_shapes=[
            pltpu.VMEM(gain.shape, gain.dtype),
            pltpu.VMEM((width, hidden), jnp.bfloat16),
            pltpu.VMEM((hidden, width), jnp.bfloat16),
            pltpu.SemaphoreType.DMA,
            pltpu.SemaphoreType.DMA((width // DEPTH,)),
            pltpu.SemaphoreType.DMA((hidden // DEPTH,)),
        ],
        name="experts",
        compiler_params=pltpu.CompilerParams(vmem_limit_bytes=32 << 20),
        cost_estimate=pl.CostEstimate(
            flops=4 * per_dev * width * hidden,
            bytes_accessed=4 * width * hidden,
            transcendentals=per_dev * hidden,
        ),
    )(recv, in_hbm(gain), in_hbm(w_in), in_hbm(w_out))


def mix_kernel(groups, combine_ref, mine_ref, other_ref, out_hbm, table, out, sems):
    rows, width = out.shape
    slots = table.shape[0]
    core = lax.axis_index("core")
    for half, ref in ((core, mine_ref), (1 - core, other_ref)):
        found = ref[...].reshape(slots // CORES, width)
        size = slots // (CORES * groups)
        for g, part in enumerate(half_rows(half, slots, groups)):
            table[part, :] = found[g * size : (g + 1) * size]
    copies = []
    for i in range(rows // TILE):
        part = pl.ds(i * TILE, TILE)
        for n in range(width // COLS):
            cols = pl.ds(n * COLS, COLS)
            mixed = jnp.dot(combine_ref[part, :], table[:, cols], preferred_element_type=jnp.float32)
            out[part, cols] = mixed.astype(jnp.bfloat16)
        copies.append(pltpu.make_async_copy(out.at[part], out_hbm.at[part], sems.at[i]))
        copies[-1].start()
    for copy in copies:
        copy.wait()


def mix(groups, combine, mine, other):
    rows, slots = combine.shape
    width = mine.shape[2]
    return pl.pallas_call(
        functools.partial(mix_kernel, groups),
        out_shape=jax.ShapeDtypeStruct((rows, width), jnp.bfloat16),
        in_specs=[pl.BlockSpec(memory_space=pltpu.VMEM)] * 3,
        out_specs=pl.BlockSpec(memory_space=pltpu.HBM),
        scratch_shapes=[
            pltpu.VMEM((slots, width), jnp.bfloat16),
            pltpu.VMEM((rows, width), jnp.bfloat16),
            pltpu.SemaphoreType.DMA((rows // TILE,)),
        ],
        name="mix",
        compiler_params=pltpu.CompilerParams(vmem_limit_bytes=32 << 20),
        cost_estimate=pl.CostEstimate(
            flops=2 * rows * slots * width, bytes_accessed=2 * rows * width, transcendentals=0
        ),
    )(combine, mine, other)


def on_device(tokens, slot_keys, norm_gain, w_in, w_out):
    groups = lax.axis_size("far")
    peers = lax.axis_size(SAME_CORE)
    swap = [(0, 1), (1, 0)]
    send, keep, logits = dispatch(groups, tokens, slot_keys)
    got = lax.ppermute(send, "core", swap)
    combine = combining(logits)
    message = merge(peers, keep, got)
    received = lax.all_to_all(message, SAME_CORE, split_axis=0, concat_axis=0, tiled=True)
    copies = experts(received, norm_gain, w_in, w_out)
    mine = lax.all_to_all(copies, SAME_CORE, split_axis=0, concat_axis=0, tiled=True)
    other = lax.ppermute(mine, "core", swap)
    return mix(groups, combine, mine, other)


def solution(mesh):
    seq, grp = mesh.devices.shape
    split = jax.sharding.Mesh(mesh.devices.reshape(seq // CORES, CORES, grp), SPLIT)
    return jax.shard_map(
        on_device,
        mesh=split,
        in_specs=(
            P(SPLIT, None),
            P(),
            P(SPLIT, None),
            P(SPLIT, None, None),
            P(SPLIT, None, None),
        ),
        out_specs=P(SPLIT, None),
        check_vma=False,
    )
```

```python
import functools

import jax
import jax.numpy as jnp
from jax import lax
from jax.experimental import pallas as pl
from jax.experimental.pallas import tpu as pltpu
from jax.sharding import PartitionSpec as P

SPLIT = ("far", "core", "grp")
SAME_CORE = ("far", "grp")
CORES = 2
LANES = 128
TILE = 256
COLS = 256
HEAD = 512
IN_CHUNKS = (384, 384)
OUT_CHUNKS = (768, 768, 640, 384)
STARTS = (4, 2)
CHUNK = 1024


def in_hbm(x):
    return pltpu.with_memory_space_constraint(x, pltpu.HBM)


def split3(x):
    hi = x.astype(jnp.bfloat16)
    rest = x - hi.astype(jnp.float32)
    mid = rest.astype(jnp.bfloat16)
    low = (rest - mid.astype(jnp.float32)).astype(jnp.bfloat16)
    return hi, mid, low


def half_rows(half, slots, groups):
    size = slots // (CORES * groups)
    return [pl.ds(pl.multiple_of((g * CORES + half) * size, size), size) for g in range(groups)]


def parts_of(peak, total):
    return [p.astype(jnp.float32) for p in (*split3(peak), *split3(total))]


def stats_of(block):
    peak = block[..., 0:1] + block[..., 1:2] + block[..., 2:3]
    total = block[..., 3:4] + block[..., 4:5] + block[..., 5:6]
    return peak, total


def dispatch_kernel(
    groups, tok_hbm, keys_hbm, gain_hbm, w_in_hbm, send_ref, keep_ref, logits_ref, gain_ref, head_ref,
    tok, keys, wt, whole, tok_sem, key_sem, head_sem,
):
    rows, width = tok.shape
    slots = keys.shape[1]
    tiles = rows // TILE
    chunks = rows // CHUNK

    def tok_copy(i):
        part = pl.ds(i * CHUNK, CHUNK)
        return pltpu.make_async_copy(tok_hbm.at[part], tok.at[part], tok_sem.at[i])

    key_copy = pltpu.make_async_copy(keys_hbm, keys, key_sem)
    key_copy.start()
    for i in range(chunks):
        tok_copy(i).start()
    key_copy.wait()
    ahead = (
        pltpu.make_async_copy(gain_hbm, gain_ref, head_sem.at[0]),
        pltpu.make_async_copy(w_in_hbm.at[0, pl.ds(0, HEAD)], head_ref, head_sem.at[1]),
    )
    peak8 = jnp.full((8, slots), -jnp.inf, jnp.float32)
    for i in range(tiles):
        if i * TILE % CHUNK == 0:
            tok_copy(i * TILE // CHUNK).wait()
            if i == 0:
                for copy in ahead:
                    copy.start()
        part = pl.ds(i * TILE, TILE)
        logits = jnp.dot(tok[part, :], keys[...], preferred_element_type=jnp.float32)
        logits_ref[part, :] = logits
        peak8 = jnp.maximum(peak8, jnp.max(logits.reshape(TILE // 8, 8, slots), axis=0))
    peak = jnp.max(peak8, axis=0, keepdims=True)
    total8 = jnp.zeros((8, slots), jnp.float32)
    for i in range(tiles):
        part = pl.ds(i * TILE, TILE)
        scores = jnp.exp(logits_ref[part, :] - peak)
        total8 = total8 + jnp.sum(scores.reshape(TILE // 8, 8, slots), axis=0)
        wt[:, part] = scores.astype(jnp.bfloat16).T
    total = jnp.sum(total8, axis=0, keepdims=True)
    stats = parts_of(peak, total)
    stats = jnp.concatenate(stats + [jnp.zeros((LANES - len(stats), slots), jnp.float32)], axis=0)
    for b in range(slots // LANES):
        part = slice(b * LANES, (b + 1) * LANES)
        whole[part, width:] = stats[:, part].T
    for n in range(width // COLS):
        part = pl.ds(n * COLS, COLS)
        whole[:, part] = jnp.dot(wt[...], tok[:, part], preferred_element_type=jnp.float32)
    core = lax.axis_index("core")
    size = slots // (CORES * groups)
    mine, other = half_rows(core, slots, groups), half_rows(1 - core, slots, groups)
    for g in range(groups):
        part = pl.ds(g * size, size)
        send_ref[part, :] = whole[other[g], :].astype(jnp.bfloat16)
        keep_ref[part, :] = whole[mine[g], :]
    for copy in ahead:
        copy.wait()


def dispatch(groups, tokens, keys, gain, w_in):
    rows, width = tokens.shape
    slots = keys.shape[1]
    half = slots // CORES
    return pl.pallas_call(
        functools.partial(dispatch_kernel, groups),
        out_shape=(
            jax.ShapeDtypeStruct((half, width + LANES), jnp.bfloat16),
            jax.ShapeDtypeStruct((half, width + LANES), jnp.float32),
            jax.ShapeDtypeStruct((rows, slots), jnp.float32),
            jax.ShapeDtypeStruct(gain.shape, gain.dtype),
            jax.ShapeDtypeStruct((HEAD, w_in.shape[2]), w_in.dtype),
        ),
        in_specs=[pl.BlockSpec(memory_space=pltpu.HBM)] * 4,
        out_specs=[pl.BlockSpec(memory_space=pltpu.VMEM)] * 5,
        scratch_shapes=[
            pltpu.VMEM((rows, width), jnp.bfloat16),
            pltpu.VMEM(keys.shape, jnp.bfloat16),
            pltpu.VMEM((slots, rows), jnp.bfloat16),
            pltpu.VMEM((slots, width + LANES), jnp.float32),
            pltpu.SemaphoreType.DMA((rows // CHUNK,)),
            pltpu.SemaphoreType.DMA,
            pltpu.SemaphoreType.DMA((2,)),
        ],
        name="dispatch",
        compiler_params=pltpu.CompilerParams(vmem_limit_bytes=32 << 20),
        cost_estimate=pl.CostEstimate(
            flops=4 * rows * width * slots,
            bytes_accessed=2 * rows * width,
            transcendentals=rows * slots,
        ),
    )(in_hbm(tokens), in_hbm(keys), in_hbm(gain), in_hbm(w_in))


def merge_kernel(keep_ref, got_ref, ready_ref, msg_ref):
    peers, per_dev, wide = msg_ref.shape
    width = wide - LANES
    size = 16
    lane = lax.broadcasted_iota(jnp.int32, (size, LANES), 1)
    for b in range(keep_ref.shape[0] // size):
        rows = pl.ds(b * size, size)
        keep_peak, keep_total = stats_of(keep_ref[rows, width:])
        got_peak, got_total = stats_of(got_ref[rows, width:].astype(jnp.float32))
        peak = jnp.maximum(keep_peak, got_peak)
        keep_factor, got_factor = jnp.exp(keep_peak - peak), jnp.exp(got_peak - peak)
        total = keep_factor * keep_total + got_factor * got_total
        numer = keep_factor * keep_ref[rows, :width] + got_factor * got_ref[rows, :width].astype(jnp.float32)
        stats = jnp.zeros((size, LANES), jnp.float32)
        for i, p in enumerate(parts_of(peak, total)):
            stats = jnp.where(lane == i, p, stats)
        for d in range(size // per_dev):
            part = slice(d * per_dev, (d + 1) * per_dev)
            msg_ref[b * (size // per_dev) + d, :, :width] = numer[part].astype(jnp.bfloat16)
            msg_ref[b * (size // per_dev) + d, :, width:] = stats[part].astype(jnp.bfloat16)


def merge(peers, keep, got, ready):
    half, wide = keep.shape
    return pl.pallas_call(
        merge_kernel,
        out_shape=jax.ShapeDtypeStruct((peers, half // peers, wide), jnp.bfloat16),
        in_specs=[pl.BlockSpec(memory_space=pltpu.VMEM)] * 3,
        out_specs=pl.BlockSpec(memory_space=pltpu.VMEM),
        name="merge",
        compiler_params=pltpu.CompilerParams(vmem_limit_bytes=32 << 20),
    )(keep, got, ready)


def combine_kernel(logits_ref, combine_ref, ready_ref):
    for i in range(logits_ref.shape[0] // TILE):
        part = pl.ds(i * TILE, TILE)
        logits = logits_ref[part, :]
        row_exp = jnp.exp(logits - jnp.max(logits, axis=1, keepdims=True))
        combine_ref[part, :] = (row_exp / jnp.sum(row_exp, axis=1, keepdims=True)).astype(jnp.bfloat16)
    ready_ref[...] = jnp.zeros_like(ready_ref)


def combining(logits):
    return pl.pallas_call(
        combine_kernel,
        out_shape=(
            jax.ShapeDtypeStruct(logits.shape, jnp.bfloat16),
            jax.ShapeDtypeStruct((8, LANES), jnp.float32),
        ),
        in_specs=[pl.BlockSpec(memory_space=pltpu.VMEM)],
        out_specs=[pl.BlockSpec(memory_space=pltpu.VMEM)] * 2,
        name="combining",
        compiler_params=pltpu.CompilerParams(vmem_limit_bytes=32 << 20),
        cost_estimate=pl.CostEstimate(
            flops=8 * logits.size, bytes_accessed=6 * logits.size, transcendentals=logits.size
        ),
    )(logits)


def expert_kernel(recv_ref, gain_ref, head_ref, w_in_hbm, w_out_hbm, out_ref, w_in, w_out, in_sem, out_sem):
    peers, per_dev, wide = recv_ref.shape
    width, hidden = w_out.shape[1], w_out.shape[0]

    def spans(sizes):
        return [(sum(sizes[:i]), size) for i, size in enumerate(sizes)]

    def copy_of(src, dst, sems, i, span, skip):
        return pltpu.make_async_copy(
            src.at[0, pl.ds(skip + span[0], span[1])], dst.at[pl.ds(*span)], sems.at[i]
        )

    in_spans, out_spans = spans(IN_CHUNKS), spans(OUT_CHUNKS)
    in_copies = [copy_of(w_in_hbm, w_in, in_sem, i, span, HEAD) for i, span in enumerate(in_spans)]
    out_copies = [copy_of(w_out_hbm, w_out, out_sem, i, span, 0) for i, span in enumerate(out_spans)]
    waiting = in_copies + out_copies
    schedule = list(STARTS)

    def start_some():
        for _ in range(schedule.pop(0) if schedule else 0):
            waiting.pop(0).start()

    start_some()

    peaks, totals = stats_of(recv_ref[:, :, width:].astype(jnp.float32))
    factor = jnp.exp(peaks - jnp.max(peaks, axis=0, keepdims=True))
    own_total = jnp.sum(totals * factor, axis=0)
    numer = jnp.zeros((per_dev, width), jnp.float32)
    for d in range(peers):
        numer = numer + recv_ref[d, :, :width].astype(jnp.float32) * factor[d]
    normed = (numer / own_total * gain_ref[...]).astype(jnp.bfloat16)
    pre = jnp.dot(normed[:, :HEAD], head_ref[...], preferred_element_type=jnp.float32)
    for copy, (first, size) in zip(in_copies, in_spans):
        copy.wait()
        start_some()
        pre = pre + jnp.dot(
            normed[:, HEAD + first : HEAD + first + size],
            w_in[first : first + size, :],
            preferred_element_type=jnp.float32,
        )
    act = jax.nn.gelu(pre).astype(jnp.bfloat16)
    acc = jnp.zeros((per_dev, width), jnp.float32)
    for copy, (first, size) in zip(out_copies, out_spans):
        part = slice(first, first + size)
        copy.wait()
        start_some()
        acc = acc + jnp.dot(act[:, part], w_out[part, :], preferred_element_type=jnp.float32)
    res = acc.astype(jnp.bfloat16)
    for d in range(peers):
        out_ref[d] = res


def experts(recv, gain, head, w_in, w_out):
    peers, per_dev, wide = recv.shape
    width, hidden = w_in.shape[1:]
    return pl.pallas_call(
        expert_kernel,
        out_shape=jax.ShapeDtypeStruct((peers, per_dev, width), jnp.bfloat16),
        in_specs=[pl.BlockSpec(memory_space=pltpu.VMEM)] * 3 + [pl.BlockSpec(memory_space=pltpu.HBM)] * 2,
        out_specs=pl.BlockSpec(memory_space=pltpu.VMEM),
        scratch_shapes=[
            pltpu.VMEM((width - HEAD, hidden), jnp.bfloat16),
            pltpu.VMEM((hidden, width), jnp.bfloat16),
            pltpu.SemaphoreType.DMA((len(IN_CHUNKS),)),
            pltpu.SemaphoreType.DMA((len(OUT_CHUNKS),)),
        ],
        name="experts",
        compiler_params=pltpu.CompilerParams(vmem_limit_bytes=32 << 20),
        cost_estimate=pl.CostEstimate(
            flops=4 * per_dev * width * hidden,
            bytes_accessed=4 * width * hidden,
            transcendentals=per_dev * hidden,
        ),
    )(recv, gain, head, in_hbm(w_in), in_hbm(w_out))


def mix_kernel(groups, combine_ref, mine_ref, other_ref, out_hbm, table, out, sems):
    rows, width = out.shape
    slots = table.shape[0]
    core = lax.axis_index("core")
    for half, ref in ((core, mine_ref), (1 - core, other_ref)):
        found = ref[...].reshape(slots // CORES, width)
        size = slots // (CORES * groups)
        for g, part in enumerate(half_rows(half, slots, groups)):
            table[part, :] = found[g * size : (g + 1) * size]
    copies = []
    for i in range(rows // TILE):
        part = pl.ds(i * TILE, TILE)
        for n in range(width // COLS):
            cols = pl.ds(n * COLS, COLS)
            mixed = jnp.dot(combine_ref[part, :], table[:, cols], preferred_element_type=jnp.float32)
            out[part, cols] = mixed.astype(jnp.bfloat16)
        copies.append(pltpu.make_async_copy(out.at[part], out_hbm.at[part], sems.at[i]))
        copies[-1].start()
    for copy in copies:
        copy.wait()


def mix(groups, combine, mine, other):
    rows, slots = combine.shape
    width = mine.shape[2]
    return pl.pallas_call(
        functools.partial(mix_kernel, groups),
        out_shape=jax.ShapeDtypeStruct((rows, width), jnp.bfloat16),
        in_specs=[pl.BlockSpec(memory_space=pltpu.VMEM)] * 3,
        out_specs=pl.BlockSpec(memory_space=pltpu.HBM),
        scratch_shapes=[
            pltpu.VMEM((slots, width), jnp.bfloat16),
            pltpu.VMEM((rows, width), jnp.bfloat16),
            pltpu.SemaphoreType.DMA((rows // TILE,)),
        ],
        name="mix",
        compiler_params=pltpu.CompilerParams(vmem_limit_bytes=32 << 20),
        cost_estimate=pl.CostEstimate(
            flops=2 * rows * slots * width, bytes_accessed=2 * rows * width, transcendentals=0
        ),
    )(combine, mine, other)


def on_device(tokens, slot_keys, norm_gain, w_in, w_out):
    groups = lax.axis_size("far")
    peers = lax.axis_size(SAME_CORE)
    swap = [(0, 1), (1, 0)]
    send, keep, logits, gain, head = dispatch(groups, tokens, slot_keys, norm_gain, w_in)
    got = lax.ppermute(send, "core", swap)
    combine, ready = combining(logits)
    message = merge(peers, keep, got, ready)
    received = lax.all_to_all(message, SAME_CORE, split_axis=0, concat_axis=0, tiled=True)
    copies = experts(received, gain, head, w_in, w_out)
    mine = lax.all_to_all(copies, SAME_CORE, split_axis=0, concat_axis=0, tiled=True)
    other = lax.ppermute(mine, "core", swap)
    return mix(groups, combine, mine, other)


def solution(mesh):
    seq, grp = mesh.devices.shape
    split = jax.sharding.Mesh(mesh.devices.reshape(seq // CORES, CORES, grp), SPLIT)
    return jax.shard_map(
        on_device,
        mesh=split,
        in_specs=(
            P(SPLIT, None),
            P(),
            P(SPLIT, None),
            P(SPLIT, None, None),
            P(SPLIT, None, None),
        ),
        out_specs=P(SPLIT, None),
        check_vma=False,
    )
```

```python
import functools

import jax
import jax.numpy as jnp
from jax import lax
from jax.experimental import pallas as pl
from jax.experimental.pallas import tpu as pltpu
from jax.sharding import PartitionSpec as P

SPLIT = ("far", "core", "grp")
SAME_CORE = ("far", "grp")
CORES = 2
LANES = 128
TILE = 256
COLS = 256
HEAD = 512
IN_CHUNKS = (384, 384)
OUT_CHUNKS = (768, 768, 640, 384)
STARTS = (4, 2)
CHUNK = 1024


def in_hbm(x):
    return pltpu.with_memory_space_constraint(x, pltpu.HBM)


def split3(x):
    hi = x.astype(jnp.bfloat16)
    rest = x - hi.astype(jnp.float32)
    mid = rest.astype(jnp.bfloat16)
    low = (rest - mid.astype(jnp.float32)).astype(jnp.bfloat16)
    return hi, mid, low


def half_rows(half, slots, groups):
    size = slots // (CORES * groups)
    return [pl.ds(pl.multiple_of((g * CORES + half) * size, size), size) for g in range(groups)]


def parts_of(peak, total):
    return [p.astype(jnp.float32) for p in (*split3(peak), *split3(total))]


def stats_of(block):
    peak = block[..., 0:1] + block[..., 1:2] + block[..., 2:3]
    total = block[..., 3:4] + block[..., 4:5] + block[..., 5:6]
    return peak, total


def dispatch_kernel(
    groups, tok_hbm, keys_hbm, gain_hbm, w_in_hbm, send_ref, keep_ref, logits_ref, gain_ref, head_ref,
    tok, keys, wt, whole, tok_sem, key_sem, head_sem,
):
    rows, width = tok.shape
    slots = keys.shape[1]
    chunks = rows // CHUNK

    def tok_copy(i):
        part = pl.ds(i * CHUNK, CHUNK)
        return pltpu.make_async_copy(tok_hbm.at[part], tok.at[part], tok_sem.at[i])

    key_copy = pltpu.make_async_copy(keys_hbm, keys, key_sem)
    key_copy.start()
    for i in range(chunks):
        tok_copy(i).start()
    key_copy.wait()
    ahead = (
        pltpu.make_async_copy(gain_hbm, gain_ref, head_sem.at[0]),
        pltpu.make_async_copy(w_in_hbm.at[0, pl.ds(0, HEAD)], head_ref, head_sem.at[1]),
    )
    folded = (TILE // 8, 8, slots)
    kinds = []
    for chunk in range(chunks):
        tok_copy(chunk).wait()
        if chunk == 0:
            for copy in ahead:
                copy.start()
        peak8 = jnp.full((8, slots), -jnp.inf, jnp.float32)
        tiles = range(chunk * CHUNK // TILE, (chunk + 1) * CHUNK // TILE)
        for i in tiles:
            part = pl.ds(i * TILE, TILE)
            logits = jnp.dot(tok[part, :], keys[...], preferred_element_type=jnp.float32)
            logits_ref[part, :] = logits
            peak8 = jnp.maximum(peak8, jnp.max(logits.reshape(folded), axis=0))
        peak = jnp.max(peak8, axis=0, keepdims=True)
        kinds.append((peak, tiles))
    top = functools.reduce(jnp.maximum, [peak for peak, _ in kinds])
    total = jnp.zeros((1, slots), jnp.float32)
    factors = []
    for peak, tiles in kinds:
        total8 = jnp.zeros((8, slots), jnp.float32)
        for i in tiles:
            part = pl.ds(i * TILE, TILE)
            scores = jnp.exp(logits_ref[part, :] - peak)
            total8 = total8 + jnp.sum(scores.reshape(folded), axis=0)
            wt[:, part] = scores.astype(jnp.bfloat16).T
        factor = jnp.exp(peak - top)
        total = total + factor * jnp.sum(total8, axis=0, keepdims=True)
        factors.append(factor)
    stats = parts_of(top, total) + factors
    stats = jnp.concatenate(stats + [jnp.zeros((LANES - len(stats), slots), jnp.float32)], axis=0)
    columns = jnp.concatenate([stats[:, b * LANES : (b + 1) * LANES].T for b in range(slots // LANES)], axis=0)
    whole[:, width:] = columns
    for c in range(chunks):
        rows_c = pl.ds(c * CHUNK, CHUNK)
        for n in range(width // COLS):
            part = pl.ds(n * COLS, COLS)
            piece = jnp.dot(wt[:, rows_c], tok[rows_c, part], preferred_element_type=jnp.float32)
            piece = piece * columns[:, 6 + c : 7 + c]
            whole[:, part] = piece if c == 0 else whole[:, part] + piece
    core = lax.axis_index("core")
    size = slots // (CORES * groups)
    mine, other = half_rows(core, slots, groups), half_rows(1 - core, slots, groups)
    for g in range(groups):
        part = pl.ds(g * size, size)
        send_ref[part, :] = whole[other[g], :].astype(jnp.bfloat16)
        keep_ref[part, :] = whole[mine[g], :]
    for copy in ahead:
        copy.wait()


def dispatch(groups, tokens, keys, gain, w_in):
    rows, width = tokens.shape
    slots = keys.shape[1]
    half = slots // CORES
    return pl.pallas_call(
        functools.partial(dispatch_kernel, groups),
        out_shape=(
            jax.ShapeDtypeStruct((half, width + LANES), jnp.bfloat16),
            jax.ShapeDtypeStruct((half, width + LANES), jnp.float32),
            jax.ShapeDtypeStruct((rows, slots), jnp.float32),
            jax.ShapeDtypeStruct(gain.shape, gain.dtype),
            jax.ShapeDtypeStruct((HEAD, w_in.shape[2]), w_in.dtype),
        ),
        in_specs=[pl.BlockSpec(memory_space=pltpu.HBM)] * 4,
        out_specs=[pl.BlockSpec(memory_space=pltpu.VMEM)] * 5,
        scratch_shapes=[
            pltpu.VMEM((rows, width), jnp.bfloat16),
            pltpu.VMEM(keys.shape, jnp.bfloat16),
            pltpu.VMEM((slots, rows), jnp.bfloat16),
            pltpu.VMEM((slots, width + LANES), jnp.float32),
            pltpu.SemaphoreType.DMA((rows // CHUNK,)),
            pltpu.SemaphoreType.DMA,
            pltpu.SemaphoreType.DMA((2,)),
        ],
        name="dispatch",
        compiler_params=pltpu.CompilerParams(vmem_limit_bytes=32 << 20),
        cost_estimate=pl.CostEstimate(
            flops=4 * rows * width * slots,
            bytes_accessed=2 * rows * width,
            transcendentals=rows * slots,
        ),
    )(in_hbm(tokens), in_hbm(keys), in_hbm(gain), in_hbm(w_in))


def merge_kernel(keep_ref, got_ref, ready_ref, msg_ref):
    peers, per_dev, wide = msg_ref.shape
    width = wide - LANES
    size = 16
    lane = lax.broadcasted_iota(jnp.int32, (size, LANES), 1)
    for b in range(keep_ref.shape[0] // size):
        rows = pl.ds(b * size, size)
        keep_peak, keep_total = stats_of(keep_ref[rows, width:])
        got_peak, got_total = stats_of(got_ref[rows, width:].astype(jnp.float32))
        peak = jnp.maximum(keep_peak, got_peak)
        keep_factor, got_factor = jnp.exp(keep_peak - peak), jnp.exp(got_peak - peak)
        total = keep_factor * keep_total + got_factor * got_total
        numer = keep_factor * keep_ref[rows, :width] + got_factor * got_ref[rows, :width].astype(jnp.float32)
        stats = jnp.zeros((size, LANES), jnp.float32)
        for i, p in enumerate(parts_of(peak, total)):
            stats = jnp.where(lane == i, p, stats)
        for d in range(size // per_dev):
            part = slice(d * per_dev, (d + 1) * per_dev)
            msg_ref[b * (size // per_dev) + d, :, :width] = numer[part].astype(jnp.bfloat16)
            msg_ref[b * (size // per_dev) + d, :, width:] = stats[part].astype(jnp.bfloat16)


def merge(peers, keep, got, ready):
    half, wide = keep.shape
    return pl.pallas_call(
        merge_kernel,
        out_shape=jax.ShapeDtypeStruct((peers, half // peers, wide), jnp.bfloat16),
        in_specs=[pl.BlockSpec(memory_space=pltpu.VMEM)] * 3,
        out_specs=pl.BlockSpec(memory_space=pltpu.VMEM),
        name="merge",
        compiler_params=pltpu.CompilerParams(vmem_limit_bytes=32 << 20),
    )(keep, got, ready)


def combine_kernel(logits_ref, combine_ref, ready_ref):
    for i in range(logits_ref.shape[0] // TILE):
        part = pl.ds(i * TILE, TILE)
        logits = logits_ref[part, :]
        row_exp = jnp.exp(logits - jnp.max(logits, axis=1, keepdims=True))
        combine_ref[part, :] = (row_exp / jnp.sum(row_exp, axis=1, keepdims=True)).astype(jnp.bfloat16)
    ready_ref[...] = jnp.zeros_like(ready_ref)


def combining(logits):
    return pl.pallas_call(
        combine_kernel,
        out_shape=(
            jax.ShapeDtypeStruct(logits.shape, jnp.bfloat16),
            jax.ShapeDtypeStruct((8, LANES), jnp.float32),
        ),
        in_specs=[pl.BlockSpec(memory_space=pltpu.VMEM)],
        out_specs=[pl.BlockSpec(memory_space=pltpu.VMEM)] * 2,
        name="combining",
        compiler_params=pltpu.CompilerParams(vmem_limit_bytes=32 << 20),
        cost_estimate=pl.CostEstimate(
            flops=8 * logits.size, bytes_accessed=6 * logits.size, transcendentals=logits.size
        ),
    )(logits)


def expert_kernel(recv_ref, gain_ref, head_ref, w_in_hbm, w_out_hbm, out_ref, w_in, w_out, in_sem, out_sem):
    peers, per_dev, wide = recv_ref.shape
    width, hidden = w_out.shape[1], w_out.shape[0]

    def spans(sizes):
        return [(sum(sizes[:i]), size) for i, size in enumerate(sizes)]

    def copy_of(src, dst, sems, i, span, skip):
        return pltpu.make_async_copy(
            src.at[0, pl.ds(skip + span[0], span[1])], dst.at[pl.ds(*span)], sems.at[i]
        )

    in_spans, out_spans = spans(IN_CHUNKS), spans(OUT_CHUNKS)
    in_copies = [copy_of(w_in_hbm, w_in, in_sem, i, span, HEAD) for i, span in enumerate(in_spans)]
    out_copies = [copy_of(w_out_hbm, w_out, out_sem, i, span, 0) for i, span in enumerate(out_spans)]
    waiting = in_copies + out_copies
    schedule = list(STARTS)

    def start_some():
        for _ in range(schedule.pop(0) if schedule else 0):
            waiting.pop(0).start()

    start_some()

    peaks, totals = stats_of(recv_ref[:, :, width:].astype(jnp.float32))
    factor = jnp.exp(peaks - jnp.max(peaks, axis=0, keepdims=True))
    own_total = jnp.sum(totals * factor, axis=0)
    numer = jnp.zeros((per_dev, width), jnp.float32)
    for d in range(peers):
        numer = numer + recv_ref[d, :, :width].astype(jnp.float32) * factor[d]
    normed = (numer / own_total * gain_ref[...]).astype(jnp.bfloat16)
    pre = jnp.dot(normed[:, :HEAD], head_ref[...], preferred_element_type=jnp.float32)
    for copy, (first, size) in zip(in_copies, in_spans):
        copy.wait()
        start_some()
        pre = pre + jnp.dot(
            normed[:, HEAD + first : HEAD + first + size],
            w_in[first : first + size, :],
            preferred_element_type=jnp.float32,
        )
    act = jax.nn.gelu(pre).astype(jnp.bfloat16)
    acc = jnp.zeros((per_dev, width), jnp.float32)
    for copy, (first, size) in zip(out_copies, out_spans):
        part = slice(first, first + size)
        copy.wait()
        start_some()
        acc = acc + jnp.dot(act[:, part], w_out[part, :], preferred_element_type=jnp.float32)
    res = acc.astype(jnp.bfloat16)
    for d in range(peers):
        out_ref[d] = res


def experts(recv, gain, head, w_in, w_out):
    peers, per_dev, wide = recv.shape
    width, hidden = w_in.shape[1:]
    return pl.pallas_call(
        expert_kernel,
        out_shape=jax.ShapeDtypeStruct((peers, per_dev, width), jnp.bfloat16),
        in_specs=[pl.BlockSpec(memory_space=pltpu.VMEM)] * 3 + [pl.BlockSpec(memory_space=pltpu.HBM)] * 2,
        out_specs=pl.BlockSpec(memory_space=pltpu.VMEM),
        scratch_shapes=[
            pltpu.VMEM((width - HEAD, hidden), jnp.bfloat16),
            pltpu.VMEM((hidden, width), jnp.bfloat16),
            pltpu.SemaphoreType.DMA((len(IN_CHUNKS),)),
            pltpu.SemaphoreType.DMA((len(OUT_CHUNKS),)),
        ],
        name="experts",
        compiler_params=pltpu.CompilerParams(vmem_limit_bytes=32 << 20),
        cost_estimate=pl.CostEstimate(
            flops=4 * per_dev * width * hidden,
            bytes_accessed=4 * width * hidden,
            transcendentals=per_dev * hidden,
        ),
    )(recv, gain, head, in_hbm(w_in), in_hbm(w_out))


def mix_kernel(groups, combine_ref, mine_ref, other_ref, out_hbm, table, out, sems):
    rows, width = out.shape
    slots = table.shape[0]
    core = lax.axis_index("core")
    for half, ref in ((core, mine_ref), (1 - core, other_ref)):
        found = ref[...].reshape(slots // CORES, width)
        size = slots // (CORES * groups)
        for g, part in enumerate(half_rows(half, slots, groups)):
            table[part, :] = found[g * size : (g + 1) * size]
    copies = []
    for i in range(rows // TILE):
        part = pl.ds(i * TILE, TILE)
        for n in range(width // COLS):
            cols = pl.ds(n * COLS, COLS)
            mixed = jnp.dot(combine_ref[part, :], table[:, cols], preferred_element_type=jnp.float32)
            out[part, cols] = mixed.astype(jnp.bfloat16)
        copies.append(pltpu.make_async_copy(out.at[part], out_hbm.at[part], sems.at[i]))
        copies[-1].start()
    for copy in copies:
        copy.wait()


def mix(groups, combine, mine, other):
    rows, slots = combine.shape
    width = mine.shape[2]
    return pl.pallas_call(
        functools.partial(mix_kernel, groups),
        out_shape=jax.ShapeDtypeStruct((rows, width), jnp.bfloat16),
        in_specs=[pl.BlockSpec(memory_space=pltpu.VMEM)] * 3,
        out_specs=pl.BlockSpec(memory_space=pltpu.HBM),
        scratch_shapes=[
            pltpu.VMEM((slots, width), jnp.bfloat16),
            pltpu.VMEM((rows, width), jnp.bfloat16),
            pltpu.SemaphoreType.DMA((rows // TILE,)),
        ],
        name="mix",
        compiler_params=pltpu.CompilerParams(vmem_limit_bytes=32 << 20),
        cost_estimate=pl.CostEstimate(
            flops=2 * rows * slots * width, bytes_accessed=2 * rows * width, transcendentals=0
        ),
    )(combine, mine, other)


def on_device(tokens, slot_keys, norm_gain, w_in, w_out):
    groups = lax.axis_size("far")
    peers = lax.axis_size(SAME_CORE)
    swap = [(0, 1), (1, 0)]
    send, keep, logits, gain, head = dispatch(groups, tokens, slot_keys, norm_gain, w_in)
    got = lax.ppermute(send, "core", swap)
    combine, ready = combining(logits)
    message = merge(peers, keep, got, ready)
    received = lax.all_to_all(message, SAME_CORE, split_axis=0, concat_axis=0, tiled=True)
    copies = experts(received, gain, head, w_in, w_out)
    mine = lax.all_to_all(copies, SAME_CORE, split_axis=0, concat_axis=0, tiled=True)
    other = lax.ppermute(mine, "core", swap)
    return mix(groups, combine, mine, other)


def solution(mesh):
    seq, grp = mesh.devices.shape
    split = jax.sharding.Mesh(mesh.devices.reshape(seq // CORES, CORES, grp), SPLIT)
    return jax.shard_map(
        on_device,
        mesh=split,
        in_specs=(
            P(SPLIT, None),
            P(),
            P(SPLIT, None),
            P(SPLIT, None, None),
            P(SPLIT, None, None),
        ),
        out_specs=P(SPLIT, None),
        check_vma=False,
    )
```

```python
import functools

import jax
import jax.numpy as jnp
from jax import lax
from jax.experimental import pallas as pl
from jax.experimental.pallas import tpu as pltpu
from jax.sharding import PartitionSpec as P

SPLIT = ("far", "core", "grp")
SAME_CORE = ("far", "grp")
CORES = 2
LANES = 128
TILE = 256
COLS = 256
HEAD = 1024
IN_CHUNKS = (128, 128)
OUT_CHUNKS = (768, 768, 640, 384)
STARTS = (4, 2)
CHUNK = 1024


def in_hbm(x):
    return pltpu.with_memory_space_constraint(x, pltpu.HBM)


def split3(x):
    hi = x.astype(jnp.bfloat16)
    rest = x - hi.astype(jnp.float32)
    mid = rest.astype(jnp.bfloat16)
    low = (rest - mid.astype(jnp.float32)).astype(jnp.bfloat16)
    return hi, mid, low


def half_rows(half, slots, groups):
    size = slots // (CORES * groups)
    return [pl.ds(pl.multiple_of((g * CORES + half) * size, size), size) for g in range(groups)]


def parts_of(peak, total):
    return [p.astype(jnp.float32) for p in (*split3(peak), *split3(total))]


def stats_of(block):
    peak = block[..., 0:1] + block[..., 1:2] + block[..., 2:3]
    total = block[..., 3:4] + block[..., 4:5] + block[..., 5:6]
    return peak, total


def dispatch_kernel(
    groups, tok_hbm, keys_hbm, gain_hbm, w_in_hbm, send_ref, keep_ref, logits_ref, gain_ref, head_ref,
    tok, keys, wt, whole, tok_sem, key_sem, head_sem,
):
    rows, width = tok.shape
    slots = keys.shape[1]
    chunks = rows // CHUNK

    def tok_copy(i):
        part = pl.ds(i * CHUNK, CHUNK)
        return pltpu.make_async_copy(tok_hbm.at[part], tok.at[part], tok_sem.at[i])

    key_copy = pltpu.make_async_copy(keys_hbm, keys, key_sem)
    key_copy.start()
    for i in range(chunks):
        tok_copy(i).start()
    key_copy.wait()
    ahead = (
        pltpu.make_async_copy(gain_hbm, gain_ref, head_sem.at[0]),
        pltpu.make_async_copy(w_in_hbm.at[0, pl.ds(0, HEAD)], head_ref, head_sem.at[1]),
    )
    folded = (TILE // 8, 8, slots)
    kinds = []
    for chunk in range(chunks):
        tok_copy(chunk).wait()
        if chunk == 0:
            for copy in ahead:
                copy.start()
        peak8 = jnp.full((8, slots), -jnp.inf, jnp.float32)
        tiles = range(chunk * CHUNK // TILE, (chunk + 1) * CHUNK // TILE)
        for i in tiles:
            part = pl.ds(i * TILE, TILE)
            logits = jnp.dot(tok[part, :], keys[...], preferred_element_type=jnp.float32)
            logits_ref[part, :] = logits
            peak8 = jnp.maximum(peak8, jnp.max(logits.reshape(folded), axis=0))
        peak = jnp.max(peak8, axis=0, keepdims=True)
        kinds.append((peak, tiles))
    top = functools.reduce(jnp.maximum, [peak for peak, _ in kinds])
    total = jnp.zeros((1, slots), jnp.float32)
    factors = []
    for peak, tiles in kinds:
        total8 = jnp.zeros((8, slots), jnp.float32)
        for i in tiles:
            part = pl.ds(i * TILE, TILE)
            scores = jnp.exp(logits_ref[part, :] - peak)
            total8 = total8 + jnp.sum(scores.reshape(folded), axis=0)
            wt[:, part] = scores.astype(jnp.bfloat16).T
        factor = jnp.exp(peak - top)
        total = total + factor * jnp.sum(total8, axis=0, keepdims=True)
        factors.append(factor)
    stats = parts_of(top, total) + factors
    stats = jnp.concatenate(stats + [jnp.zeros((LANES - len(stats), slots), jnp.float32)], axis=0)
    columns = jnp.concatenate([stats[:, b * LANES : (b + 1) * LANES].T for b in range(slots // LANES)], axis=0)
    whole[:, width:] = columns
    for c in range(chunks):
        rows_c = pl.ds(c * CHUNK, CHUNK)
        for n in range(width // COLS):
            part = pl.ds(n * COLS, COLS)
            piece = jnp.dot(wt[:, rows_c], tok[rows_c, part], preferred_element_type=jnp.float32)
            piece = piece * columns[:, 6 + c : 7 + c]
            whole[:, part] = piece if c == 0 else whole[:, part] + piece
    core = lax.axis_index("core")
    size = slots // (CORES * groups)
    mine, other = half_rows(core, slots, groups), half_rows(1 - core, slots, groups)
    for g in range(groups):
        part = pl.ds(g * size, size)
        send_ref[part, :] = whole[other[g], :].astype(jnp.bfloat16)
        keep_ref[part, :] = whole[mine[g], :]
    for copy in ahead:
        copy.wait()


def dispatch(groups, tokens, keys, gain, w_in):
    rows, width = tokens.shape
    slots = keys.shape[1]
    half = slots // CORES
    return pl.pallas_call(
        functools.partial(dispatch_kernel, groups),
        out_shape=(
            jax.ShapeDtypeStruct((half, width + LANES), jnp.bfloat16),
            jax.ShapeDtypeStruct((half, width + LANES), jnp.float32),
            jax.ShapeDtypeStruct((rows, slots), jnp.float32),
            jax.ShapeDtypeStruct(gain.shape, gain.dtype),
            jax.ShapeDtypeStruct((HEAD, w_in.shape[2]), w_in.dtype),
        ),
        in_specs=[pl.BlockSpec(memory_space=pltpu.HBM)] * 4,
        out_specs=[pl.BlockSpec(memory_space=pltpu.VMEM)] * 5,
        scratch_shapes=[
            pltpu.VMEM((rows, width), jnp.bfloat16),
            pltpu.VMEM(keys.shape, jnp.bfloat16),
            pltpu.VMEM((slots, rows), jnp.bfloat16),
            pltpu.VMEM((slots, width + LANES), jnp.float32),
            pltpu.SemaphoreType.DMA((rows // CHUNK,)),
            pltpu.SemaphoreType.DMA,
            pltpu.SemaphoreType.DMA((2,)),
        ],
        name="dispatch",
        compiler_params=pltpu.CompilerParams(vmem_limit_bytes=32 << 20),
        cost_estimate=pl.CostEstimate(
            flops=4 * rows * width * slots,
            bytes_accessed=2 * rows * width,
            transcendentals=rows * slots,
        ),
    )(in_hbm(tokens), in_hbm(keys), in_hbm(gain), in_hbm(w_in))


def merge_kernel(keep_ref, got_ref, ready_ref, msg_ref):
    peers, per_dev, wide = msg_ref.shape
    width = wide - LANES
    size = 16
    lane = lax.broadcasted_iota(jnp.int32, (size, LANES), 1)
    for b in range(keep_ref.shape[0] // size):
        rows = pl.ds(b * size, size)
        keep_peak, keep_total = stats_of(keep_ref[rows, width:])
        got_peak, got_total = stats_of(got_ref[rows, width:].astype(jnp.float32))
        peak = jnp.maximum(keep_peak, got_peak)
        keep_factor, got_factor = jnp.exp(keep_peak - peak), jnp.exp(got_peak - peak)
        total = keep_factor * keep_total + got_factor * got_total
        numer = keep_factor * keep_ref[rows, :width] + got_factor * got_ref[rows, :width].astype(jnp.float32)
        stats = jnp.zeros((size, LANES), jnp.float32)
        for i, p in enumerate(parts_of(peak, total)):
            stats = jnp.where(lane == i, p, stats)
        for d in range(size // per_dev):
            part = slice(d * per_dev, (d + 1) * per_dev)
            msg_ref[b * (size // per_dev) + d, :, :width] = numer[part].astype(jnp.bfloat16)
            msg_ref[b * (size // per_dev) + d, :, width:] = stats[part].astype(jnp.bfloat16)


def merge(peers, keep, got, ready):
    half, wide = keep.shape
    return pl.pallas_call(
        merge_kernel,
        out_shape=jax.ShapeDtypeStruct((peers, half // peers, wide), jnp.bfloat16),
        in_specs=[pl.BlockSpec(memory_space=pltpu.VMEM)] * 3,
        out_specs=pl.BlockSpec(memory_space=pltpu.VMEM),
        name="merge",
        compiler_params=pltpu.CompilerParams(vmem_limit_bytes=32 << 20),
    )(keep, got, ready)


def combine_kernel(logits_ref, combine_ref, ready_ref):
    for i in range(logits_ref.shape[0] // TILE):
        part = pl.ds(i * TILE, TILE)
        logits = logits_ref[part, :]
        row_exp = jnp.exp(logits - jnp.max(logits, axis=1, keepdims=True))
        combine_ref[part, :] = (row_exp / jnp.sum(row_exp, axis=1, keepdims=True)).astype(jnp.bfloat16)
    ready_ref[...] = jnp.zeros_like(ready_ref)


def combining(logits):
    return pl.pallas_call(
        combine_kernel,
        out_shape=(
            jax.ShapeDtypeStruct(logits.shape, jnp.bfloat16),
            jax.ShapeDtypeStruct((8, LANES), jnp.float32),
        ),
        in_specs=[pl.BlockSpec(memory_space=pltpu.VMEM)],
        out_specs=[pl.BlockSpec(memory_space=pltpu.VMEM)] * 2,
        name="combining",
        compiler_params=pltpu.CompilerParams(vmem_limit_bytes=32 << 20),
        cost_estimate=pl.CostEstimate(
            flops=8 * logits.size, bytes_accessed=6 * logits.size, transcendentals=logits.size
        ),
    )(logits)


def expert_kernel(recv_ref, gain_ref, head_ref, w_in_hbm, w_out_hbm, out_ref, w_in, w_out, in_sem, out_sem):
    peers, per_dev, wide = recv_ref.shape
    width, hidden = w_out.shape[1], w_out.shape[0]

    def spans(sizes):
        return [(sum(sizes[:i]), size) for i, size in enumerate(sizes)]

    def copy_of(src, dst, sems, i, span, skip):
        return pltpu.make_async_copy(
            src.at[0, pl.ds(skip + span[0], span[1])], dst.at[pl.ds(*span)], sems.at[i]
        )

    in_spans, out_spans = spans(IN_CHUNKS), spans(OUT_CHUNKS)
    in_copies = [copy_of(w_in_hbm, w_in, in_sem, i, span, HEAD) for i, span in enumerate(in_spans)]
    out_copies = [copy_of(w_out_hbm, w_out, out_sem, i, span, 0) for i, span in enumerate(out_spans)]
    waiting = in_copies + out_copies
    schedule = list(STARTS)

    def start_some():
        for _ in range(schedule.pop(0) if schedule else 0):
            waiting.pop(0).start()

    start_some()

    peaks, totals = stats_of(recv_ref[:, :, width:].astype(jnp.float32))
    factor = jnp.exp(peaks - jnp.max(peaks, axis=0, keepdims=True))
    own_total = jnp.sum(totals * factor, axis=0)
    numer = jnp.zeros((per_dev, width), jnp.float32)
    for d in range(peers):
        numer = numer + recv_ref[d, :, :width].astype(jnp.float32) * factor[d]
    normed = (numer / own_total * gain_ref[...]).astype(jnp.bfloat16)
    pre = jnp.dot(normed[:, :HEAD], head_ref[...], preferred_element_type=jnp.float32)
    for copy, (first, size) in zip(in_copies, in_spans):
        copy.wait()
        start_some()
        pre = pre + jnp.dot(
            normed[:, HEAD + first : HEAD + first + size],
            w_in[first : first + size, :],
            preferred_element_type=jnp.float32,
        )
    act = jax.nn.gelu(pre).astype(jnp.bfloat16)
    acc = jnp.zeros((per_dev, width), jnp.float32)
    for copy, (first, size) in zip(out_copies, out_spans):
        part = slice(first, first + size)
        copy.wait()
        start_some()
        acc = acc + jnp.dot(act[:, part], w_out[part, :], preferred_element_type=jnp.float32)
    res = acc.astype(jnp.bfloat16)
    for d in range(peers):
        out_ref[d] = res


def experts(recv, gain, head, w_in, w_out):
    peers, per_dev, wide = recv.shape
    width, hidden = w_in.shape[1:]
    return pl.pallas_call(
        expert_kernel,
        out_shape=jax.ShapeDtypeStruct((peers, per_dev, width), jnp.bfloat16),
        in_specs=[pl.BlockSpec(memory_space=pltpu.VMEM)] * 3 + [pl.BlockSpec(memory_space=pltpu.HBM)] * 2,
        out_specs=pl.BlockSpec(memory_space=pltpu.VMEM),
        scratch_shapes=[
            pltpu.VMEM((width - HEAD, hidden), jnp.bfloat16),
            pltpu.VMEM((hidden, width), jnp.bfloat16),
            pltpu.SemaphoreType.DMA((len(IN_CHUNKS),)),
            pltpu.SemaphoreType.DMA((len(OUT_CHUNKS),)),
        ],
        name="experts",
        compiler_params=pltpu.CompilerParams(vmem_limit_bytes=32 << 20),
        cost_estimate=pl.CostEstimate(
            flops=4 * per_dev * width * hidden,
            bytes_accessed=4 * width * hidden,
            transcendentals=per_dev * hidden,
        ),
    )(recv, gain, head, in_hbm(w_in), in_hbm(w_out))


def mix_kernel(groups, combine_ref, mine_ref, other_ref, out_hbm, table, out, sems):
    rows, width = out.shape
    slots = table.shape[0]
    core = lax.axis_index("core")
    for half, ref in ((core, mine_ref), (1 - core, other_ref)):
        found = ref[...].reshape(slots // CORES, width)
        size = slots // (CORES * groups)
        for g, part in enumerate(half_rows(half, slots, groups)):
            table[part, :] = found[g * size : (g + 1) * size]
    copies = []
    for i in range(rows // TILE):
        part = pl.ds(i * TILE, TILE)
        for n in range(width // COLS):
            cols = pl.ds(n * COLS, COLS)
            mixed = jnp.dot(combine_ref[part, :], table[:, cols], preferred_element_type=jnp.float32)
            out[part, cols] = mixed.astype(jnp.bfloat16)
        copies.append(pltpu.make_async_copy(out.at[part], out_hbm.at[part], sems.at[i]))
        copies[-1].start()
    for copy in copies:
        copy.wait()


def mix(groups, combine, mine, other):
    rows, slots = combine.shape
    width = mine.shape[2]
    return pl.pallas_call(
        functools.partial(mix_kernel, groups),
        out_shape=jax.ShapeDtypeStruct((rows, width), jnp.bfloat16),
        in_specs=[pl.BlockSpec(memory_space=pltpu.VMEM)] * 3,
        out_specs=pl.BlockSpec(memory_space=pltpu.HBM),
        scratch_shapes=[
            pltpu.VMEM((slots, width), jnp.bfloat16),
            pltpu.VMEM((rows, width), jnp.bfloat16),
            pltpu.SemaphoreType.DMA((rows // TILE,)),
        ],
        name="mix",
        compiler_params=pltpu.CompilerParams(vmem_limit_bytes=32 << 20),
        cost_estimate=pl.CostEstimate(
            flops=2 * rows * slots * width, bytes_accessed=2 * rows * width, transcendentals=0
        ),
    )(combine, mine, other)


def on_device(tokens, slot_keys, norm_gain, w_in, w_out):
    groups = lax.axis_size("far")
    peers = lax.axis_size(SAME_CORE)
    swap = [(0, 1), (1, 0)]
    send, keep, logits, gain, head = dispatch(groups, tokens, slot_keys, norm_gain, w_in)
    got = lax.ppermute(send, "core", swap)
    combine, ready = combining(logits)
    message = merge(peers, keep, got, ready)
    received = lax.all_to_all(message, SAME_CORE, split_axis=0, concat_axis=0, tiled=True)
    copies = experts(received, gain, head, w_in, w_out)
    mine = lax.all_to_all(copies, SAME_CORE, split_axis=0, concat_axis=0, tiled=True)
    other = lax.ppermute(mine, "core", swap)
    return mix(groups, combine, mine, other)


def solution(mesh):
    seq, grp = mesh.devices.shape
    split = jax.sharding.Mesh(mesh.devices.reshape(seq // CORES, CORES, grp), SPLIT)
    return jax.shard_map(
        on_device,
        mesh=split,
        in_specs=(
            P(SPLIT, None),
            P(),
            P(SPLIT, None),
            P(SPLIT, None, None),
            P(SPLIT, None, None),
        ),
        out_specs=P(SPLIT, None),
        check_vma=False,
    )
```

```python
import functools

import jax
import jax.numpy as jnp
from jax import lax
from jax.experimental import pallas as pl
from jax.experimental.pallas import tpu as pltpu
from jax.sharding import PartitionSpec as P

SPLIT = ("far", "core", "grp")
SAME_CORE = ("far", "grp")
CORES = 2
LANES = 128
TILE = 256
COLS = 256
HEAD = 1152
IN_CHUNKS = (64, 64)
OUT_CHUNKS = (768, 768, 640, 384)
STARTS = (4, 2)
CHUNK = 1024


def in_hbm(x):
    return pltpu.with_memory_space_constraint(x, pltpu.HBM)


def split3(x):
    hi = x.astype(jnp.bfloat16)
    rest = x - hi.astype(jnp.float32)
    mid = rest.astype(jnp.bfloat16)
    low = (rest - mid.astype(jnp.float32)).astype(jnp.bfloat16)
    return hi, mid, low


def half_rows(half, slots, groups):
    size = slots // (CORES * groups)
    return [pl.ds(pl.multiple_of((g * CORES + half) * size, size), size) for g in range(groups)]


def parts_of(peak, total):
    return [p.astype(jnp.float32) for p in (*split3(peak), *split3(total))]


def stats_of(block):
    peak = block[..., 0:1] + block[..., 1:2] + block[..., 2:3]
    total = block[..., 3:4] + block[..., 4:5] + block[..., 5:6]
    return peak, total


def dispatch_kernel(
    groups, tok_hbm, keys_hbm, gain_hbm, w_in_hbm, send_ref, keep_ref, logits_ref, gain_ref, head_ref,
    tok, keys, wt, whole, tok_sem, key_sem, head_sem,
):
    rows, width = tok.shape
    slots = keys.shape[1]
    chunks = rows // CHUNK

    def tok_copy(i):
        part = pl.ds(i * CHUNK, CHUNK)
        return pltpu.make_async_copy(tok_hbm.at[part], tok.at[part], tok_sem.at[i])

    key_copy = pltpu.make_async_copy(keys_hbm, keys, key_sem)
    key_copy.start()
    for i in range(chunks):
        tok_copy(i).start()
    key_copy.wait()
    ahead = (
        pltpu.make_async_copy(gain_hbm, gain_ref, head_sem.at[0]),
        pltpu.make_async_copy(w_in_hbm.at[0, pl.ds(0, HEAD)], head_ref, head_sem.at[1]),
    )
    for copy in ahead:
        copy.start()
    folded = (TILE // 8, 8, slots)
    kinds = []
    for chunk in range(chunks):
        tok_copy(chunk).wait()
        peak8 = jnp.full((8, slots), -jnp.inf, jnp.float32)
        tiles = range(chunk * CHUNK // TILE, (chunk + 1) * CHUNK // TILE)
        for i in tiles:
            part = pl.ds(i * TILE, TILE)
            logits = jnp.dot(tok[part, :], keys[...], preferred_element_type=jnp.float32)
            logits_ref[part, :] = logits
            peak8 = jnp.maximum(peak8, jnp.max(logits.reshape(folded), axis=0))
        peak = jnp.max(peak8, axis=0, keepdims=True)
        kinds.append((peak, tiles))
    top = functools.reduce(jnp.maximum, [peak for peak, _ in kinds])
    total = jnp.zeros((1, slots), jnp.float32)
    factors = []
    for peak, tiles in kinds:
        total8 = jnp.zeros((8, slots), jnp.float32)
        for i in tiles:
            part = pl.ds(i * TILE, TILE)
            scores = jnp.exp(logits_ref[part, :] - peak)
            total8 = total8 + jnp.sum(scores.reshape(folded), axis=0)
            wt[:, part] = scores.astype(jnp.bfloat16).T
        factor = jnp.exp(peak - top)
        total = total + factor * jnp.sum(total8, axis=0, keepdims=True)
        factors.append(factor)
    stats = parts_of(top, total) + factors
    stats = jnp.concatenate(stats + [jnp.zeros((LANES - len(stats), slots), jnp.float32)], axis=0)
    columns = jnp.concatenate([stats[:, b * LANES : (b + 1) * LANES].T for b in range(slots // LANES)], axis=0)
    whole[:, width:] = columns
    for c in range(chunks):
        rows_c = pl.ds(c * CHUNK, CHUNK)
        for n in range(width // COLS):
            part = pl.ds(n * COLS, COLS)
            piece = jnp.dot(wt[:, rows_c], tok[rows_c, part], preferred_element_type=jnp.float32)
            piece = piece * columns[:, 6 + c : 7 + c]
            whole[:, part] = piece if c == 0 else whole[:, part] + piece
    core = lax.axis_index("core")
    size = slots // (CORES * groups)
    mine, other = half_rows(core, slots, groups), half_rows(1 - core, slots, groups)
    for g in range(groups):
        part = pl.ds(g * size, size)
        send_ref[part, :] = whole[other[g], :].astype(jnp.bfloat16)
        keep_ref[part, :] = whole[mine[g], :]
    for copy in ahead:
        copy.wait()


def dispatch(groups, tokens, keys, gain, w_in):
    rows, width = tokens.shape
    slots = keys.shape[1]
    half = slots // CORES
    return pl.pallas_call(
        functools.partial(dispatch_kernel, groups),
        out_shape=(
            jax.ShapeDtypeStruct((half, width + LANES), jnp.bfloat16),
            jax.ShapeDtypeStruct((half, width + LANES), jnp.float32),
            jax.ShapeDtypeStruct((rows, slots), jnp.float32),
            jax.ShapeDtypeStruct(gain.shape, gain.dtype),
            jax.ShapeDtypeStruct((HEAD, w_in.shape[2]), w_in.dtype),
        ),
        in_specs=[pl.BlockSpec(memory_space=pltpu.HBM)] * 4,
        out_specs=[pl.BlockSpec(memory_space=pltpu.VMEM)] * 5,
        scratch_shapes=[
            pltpu.VMEM((rows, width), jnp.bfloat16),
            pltpu.VMEM(keys.shape, jnp.bfloat16),
            pltpu.VMEM((slots, rows), jnp.bfloat16),
            pltpu.VMEM((slots, width + LANES), jnp.float32),
            pltpu.SemaphoreType.DMA((rows // CHUNK,)),
            pltpu.SemaphoreType.DMA,
            pltpu.SemaphoreType.DMA((2,)),
        ],
        name="dispatch",
        compiler_params=pltpu.CompilerParams(vmem_limit_bytes=32 << 20),
        cost_estimate=pl.CostEstimate(
            flops=4 * rows * width * slots,
            bytes_accessed=2 * rows * width,
            transcendentals=rows * slots,
        ),
    )(in_hbm(tokens), in_hbm(keys), in_hbm(gain), in_hbm(w_in))


def merge_kernel(keep_ref, got_ref, ready_ref, msg_ref):
    peers, per_dev, wide = msg_ref.shape
    width = wide - LANES
    size = 32
    lane = lax.broadcasted_iota(jnp.int32, (size, LANES), 1)
    for b in range(keep_ref.shape[0] // size):
        rows = pl.ds(b * size, size)
        keep_peak, keep_total = stats_of(keep_ref[rows, width:])
        got_peak, got_total = stats_of(got_ref[rows, width:].astype(jnp.float32))
        peak = jnp.maximum(keep_peak, got_peak)
        keep_factor, got_factor = jnp.exp(keep_peak - peak), jnp.exp(got_peak - peak)
        total = keep_factor * keep_total + got_factor * got_total
        numer = keep_factor * keep_ref[rows, :width] + got_factor * got_ref[rows, :width].astype(jnp.float32)
        stats = jnp.zeros((size, LANES), jnp.float32)
        for i, p in enumerate(parts_of(peak, total)):
            stats = jnp.where(lane == i, p, stats)
        for d in range(size // per_dev):
            part = slice(d * per_dev, (d + 1) * per_dev)
            msg_ref[b * (size // per_dev) + d, :, :width] = numer[part].astype(jnp.bfloat16)
            msg_ref[b * (size // per_dev) + d, :, width:] = stats[part].astype(jnp.bfloat16)


def merge(peers, keep, got, ready):
    half, wide = keep.shape
    return pl.pallas_call(
        merge_kernel,
        out_shape=jax.ShapeDtypeStruct((peers, half // peers, wide), jnp.bfloat16),
        in_specs=[pl.BlockSpec(memory_space=pltpu.VMEM)] * 3,
        out_specs=pl.BlockSpec(memory_space=pltpu.VMEM),
        name="merge",
        compiler_params=pltpu.CompilerParams(vmem_limit_bytes=32 << 20),
    )(keep, got, ready)


def combine_kernel(logits_ref, combine_ref, ready_ref):
    for i in range(logits_ref.shape[0] // TILE):
        part = pl.ds(i * TILE, TILE)
        logits = logits_ref[part, :]
        row_exp = jnp.exp(logits - jnp.max(logits, axis=1, keepdims=True))
        combine_ref[part, :] = (row_exp / jnp.sum(row_exp, axis=1, keepdims=True)).astype(jnp.bfloat16)
    ready_ref[...] = jnp.zeros_like(ready_ref)


def combining(logits):
    return pl.pallas_call(
        combine_kernel,
        out_shape=(
            jax.ShapeDtypeStruct(logits.shape, jnp.bfloat16),
            jax.ShapeDtypeStruct((8, LANES), jnp.float32),
        ),
        in_specs=[pl.BlockSpec(memory_space=pltpu.VMEM)],
        out_specs=[pl.BlockSpec(memory_space=pltpu.VMEM)] * 2,
        name="combining",
        compiler_params=pltpu.CompilerParams(vmem_limit_bytes=32 << 20),
        cost_estimate=pl.CostEstimate(
            flops=8 * logits.size, bytes_accessed=6 * logits.size, transcendentals=logits.size
        ),
    )(logits)


def expert_kernel(recv_ref, gain_ref, head_ref, w_in_hbm, w_out_hbm, out_ref, w_in, w_out, in_sem, out_sem):
    peers, per_dev, wide = recv_ref.shape
    width, hidden = w_out.shape[1], w_out.shape[0]

    def spans(sizes):
        return [(sum(sizes[:i]), size) for i, size in enumerate(sizes)]

    def copy_of(src, dst, sems, i, span, skip):
        return pltpu.make_async_copy(
            src.at[0, pl.ds(skip + span[0], span[1])], dst.at[pl.ds(*span)], sems.at[i]
        )

    in_spans, out_spans = spans(IN_CHUNKS), spans(OUT_CHUNKS)
    in_copies = [copy_of(w_in_hbm, w_in, in_sem, i, span, HEAD) for i, span in enumerate(in_spans)]
    out_copies = [copy_of(w_out_hbm, w_out, out_sem, i, span, 0) for i, span in enumerate(out_spans)]
    waiting = in_copies + out_copies
    schedule = list(STARTS)

    def start_some():
        for _ in range(schedule.pop(0) if schedule else 0):
            waiting.pop(0).start()

    start_some()

    peaks, totals = stats_of(recv_ref[:, :, width:].astype(jnp.float32))
    factor = jnp.exp(peaks - jnp.max(peaks, axis=0, keepdims=True))
    own_total = jnp.sum(totals * factor, axis=0)
    numer = jnp.zeros((per_dev, width), jnp.float32)
    for d in range(peers):
        numer = numer + recv_ref[d, :, :width].astype(jnp.float32) * factor[d]
    normed = (numer / own_total * gain_ref[...]).astype(jnp.bfloat16)
    pre = jnp.dot(normed[:, :HEAD], head_ref[...], preferred_element_type=jnp.float32)
    for copy, (first, size) in zip(in_copies, in_spans):
        copy.wait()
        start_some()
        pre = pre + jnp.dot(
            normed[:, HEAD + first : HEAD + first + size],
            w_in[first : first + size, :],
            preferred_element_type=jnp.float32,
        )
    act = jax.nn.gelu(pre).astype(jnp.bfloat16)
    acc = jnp.zeros((per_dev, width), jnp.float32)
    for copy, (first, size) in zip(out_copies, out_spans):
        part = slice(first, first + size)
        copy.wait()
        start_some()
        acc = acc + jnp.dot(act[:, part], w_out[part, :], preferred_element_type=jnp.float32)
    res = acc.astype(jnp.bfloat16)
    for d in range(peers):
        out_ref[d] = res


def experts(recv, gain, head, w_in, w_out):
    peers, per_dev, wide = recv.shape
    width, hidden = w_in.shape[1:]
    return pl.pallas_call(
        expert_kernel,
        out_shape=jax.ShapeDtypeStruct((peers, per_dev, width), jnp.bfloat16),
        in_specs=[pl.BlockSpec(memory_space=pltpu.VMEM)] * 3 + [pl.BlockSpec(memory_space=pltpu.HBM)] * 2,
        out_specs=pl.BlockSpec(memory_space=pltpu.VMEM),
        scratch_shapes=[
            pltpu.VMEM((width - HEAD, hidden), jnp.bfloat16),
            pltpu.VMEM((hidden, width), jnp.bfloat16),
            pltpu.SemaphoreType.DMA((len(IN_CHUNKS),)),
            pltpu.SemaphoreType.DMA((len(OUT_CHUNKS),)),
        ],
        name="experts",
        compiler_params=pltpu.CompilerParams(vmem_limit_bytes=32 << 20),
        cost_estimate=pl.CostEstimate(
            flops=4 * per_dev * width * hidden,
            bytes_accessed=4 * width * hidden,
            transcendentals=per_dev * hidden,
        ),
    )(recv, gain, head, in_hbm(w_in), in_hbm(w_out))


def flatten_kernel(rows_ref, flat_ref):
    flat_ref[...] = rows_ref[...].reshape(flat_ref.shape)


def flatten(rows):
    shape = (rows.shape[0] * rows.shape[1], rows.shape[2])
    return pl.pallas_call(
        flatten_kernel,
        out_shape=jax.ShapeDtypeStruct(shape, rows.dtype),
        in_specs=[pl.BlockSpec(memory_space=pltpu.VMEM)],
        out_specs=pl.BlockSpec(memory_space=pltpu.VMEM),
        name="flatten",
        compiler_params=pltpu.CompilerParams(vmem_limit_bytes=16 << 20),
        cost_estimate=pl.CostEstimate(flops=rows.size, bytes_accessed=4 * rows.size, transcendentals=0),
    )(rows)


def mix_kernel(groups, combine_ref, mine_ref, other_ref, out_hbm, table, out, sems):
    rows, width = out.shape
    slots = table.shape[0]
    core = lax.axis_index("core")
    for half, ref in ((core, mine_ref), (1 - core, other_ref)):
        found = ref[...].reshape(slots // CORES, width)
        size = slots // (CORES * groups)
        for g, part in enumerate(half_rows(half, slots, groups)):
            table[part, :] = found[g * size : (g + 1) * size]
    copies = []
    for i in range(rows // TILE):
        part = pl.ds(i * TILE, TILE)
        for n in range(width // COLS):
            cols = pl.ds(n * COLS, COLS)
            mixed = jnp.dot(combine_ref[part, :], table[:, cols], preferred_element_type=jnp.float32)
            out[part, cols] = mixed.astype(jnp.bfloat16)
        copies.append(pltpu.make_async_copy(out.at[part], out_hbm.at[part], sems.at[i]))
        copies[-1].start()
    for copy in copies:
        copy.wait()


def mix(groups, combine, mine, other):
    rows, slots = combine.shape
    width = mine.shape[1]
    return pl.pallas_call(
        functools.partial(mix_kernel, groups),
        out_shape=jax.ShapeDtypeStruct((rows, width), jnp.bfloat16),
        in_specs=[pl.BlockSpec(memory_space=pltpu.VMEM)] * 3,
        out_specs=pl.BlockSpec(memory_space=pltpu.HBM),
        scratch_shapes=[
            pltpu.VMEM((slots, width), jnp.bfloat16),
            pltpu.VMEM((rows, width), jnp.bfloat16),
            pltpu.SemaphoreType.DMA((rows // TILE,)),
        ],
        name="mix",
        compiler_params=pltpu.CompilerParams(vmem_limit_bytes=32 << 20),
        cost_estimate=pl.CostEstimate(
            flops=2 * rows * slots * width, bytes_accessed=2 * rows * width, transcendentals=0
        ),
    )(combine, mine, other)


def on_device(tokens, slot_keys, norm_gain, w_in, w_out):
    groups = lax.axis_size("far")
    peers = lax.axis_size(SAME_CORE)
    swap = [(0, 1), (1, 0)]
    send, keep, logits, gain, head = dispatch(groups, tokens, slot_keys, norm_gain, w_in)
    got = lax.ppermute(send, "core", swap)
    combine, ready = combining(logits)
    message = merge(peers, keep, got, ready)
    received = lax.all_to_all(message, SAME_CORE, split_axis=0, concat_axis=0, tiled=True)
    copies = experts(received, gain, head, w_in, w_out)
    mine = lax.all_to_all(copies, SAME_CORE, split_axis=0, concat_axis=0, tiled=True)
    other = lax.ppermute(mine, "core", swap)
    return mix(groups, combine, flatten(mine), other)


def solution(mesh):
    seq, grp = mesh.devices.shape
    split = jax.sharding.Mesh(mesh.devices.reshape(seq // CORES, CORES, grp), SPLIT)
    return jax.shard_map(
        on_device,
        mesh=split,
        in_specs=(
            P(SPLIT, None),
            P(),
            P(SPLIT, None),
            P(SPLIT, None, None),
            P(SPLIT, None, None),
        ),
        out_specs=P(SPLIT, None),
        check_vma=False,
    )
```
